32 devices in a mesh: expert: 8 (over z, x), dp: 4 (over y, core).
Axes of the slice: x: 2, y: 2, z: 4, core: 2. Of those that a mesh axis runs over, the one named last changes fastest.
Arguments:
- features: bfloat16 [4096, 32, 64], P(('expert', 'dp')), may hold values from -1 to 1
- spacing: float32 [4096, 32], P(('expert', 'dp')), may hold values from 0.02 to 0.3
- targets: float32 [3, 4096], P(None, ('expert', 'dp')), may hold values from 0 to 1
- ray_length: int32 [4096], P(('expert', 'dp')), may hold values from 1 to 32, as said below
- cell_id: int32 [4096, 32], P(('expert', 'dp')), may hold values from 0 to 15, as said below
- slot_rank: int32 [4096, 32], P(('expert', 'dp')), may hold values from -1 to 383, as said below
- image_id: int32 [4096], P(('expert', 'dp')), may hold values from 0 to 511, as said below
- params: float32 [16, 848, 256], P('expert'), may hold values from -5 to 5
- first_moment: float32 [16, 848, 256], P('expert'), may hold values from -0.75 to 0.75
- second_moment: float32 [16, 848, 256], P('expert'), may hold values from 1e-06 to 0.01
- code_table: float32 [512, 64], P(('expert', 'dp')), may hold values from -6 to 6
- table_first: float32 [512, 64], P(('expert', 'dp')), may hold values from -0.75 to 0.75
- table_second: float32 [512, 64], P(('expert', 'dp')), may hold values from 1e-06 to 0.01
Outputs:
- ray_loss: float32 [4096], P(('expert', 'dp'))
- new_params: float32 [16, 848, 256], P('expert')
- new_first_moment: float32 [16, 848, 256], P('expert')
- new_second_moment: float32 [16, 848, 256], P('expert')
- new_code_table: float32 [512, 64], P(('expert', 'dp'))
- new_table_first: float32 [512, 64], P(('expert', 'dp'))
- new_table_second: float32 [512, 64], P(('expert', 'dp'))
The draws below stay inside these ranges and needn't reach their ends.
Inputs may be any that keep to these rules, and one draw needn't show every extreme that they name: `ray_length`: rays form aligned blocks of 128, one a device, in the order of the axes expert then dp. In every block the lengths sum to 3072 and some ray has all 32 samples. `cell_id`: also given for samples at or beyond their ray's length, where it is unused. `slot_rank`: for a sample below its ray's length: its rank among the live samples of its block of 128 rays that have the same cell_id, counted ray by ray and along each ray; -1 for the other samples. No block has more than 384 live samples of one cell_id; in every block some cell_id has exactly 384, and one cell_id has 384 in every block. `image_id`: A ray of block b names an image from b * 16 to (b + 1) * 16 - 1.
All inputs are finite; a program needn't handle non-finite values.
Results may differ from the reference program's by a relative error of at most 0.0046.
Values may be sent and summed in bfloat16 or wider, within the bound.
A program may use at most 128 MiB of HBM per device.

```python
import math
import jax
import jax.numpy as jnp
from jax import lax

NET_WIDTH = 256
CODE_WIDTH = 64
ENC_WIDTH = 64
LAYERS = 4
SAMPLES = 32
IMG_DEV = 16
RAY_DEV = 128
EXPERTS = 16
RAY_TOTAL = 4096
IMAGES = 512
LIVE_DEV = 3072
CAPACITY = 384
PARAM_ROWS = 848


def sample_layout(key):
    blocks = RAY_TOTAL // RAY_DEV
    hot_all = jax.random.randint(jax.random.fold_in(key, 11), (), 0, EXPERTS)

    def one_block(block_number):
        subkeys = jax.random.split(jax.random.fold_in(key, block_number), 7)
        drop_units = RAY_DEV * (SAMPLES - 1)
        unit_ray = jnp.arange(drop_units, dtype=jnp.int32) // (SAMPLES - 1)
        full_ray = jax.random.randint(subkeys[0], (), 0, RAY_DEV)
        shuffled = jax.random.permutation(subkeys[1], drop_units).astype(jnp.int32)
        ranking = shuffled + jnp.where(unit_ray == full_ray, drop_units, 0).astype(jnp.int32)
        picked = jnp.argsort(ranking)[:RAY_DEV * SAMPLES // 4]
        dropped = jnp.zeros((RAY_DEV,), jnp.int32).at[unit_ray[picked]].add(1)
        lengths = (SAMPLES - dropped).astype(jnp.int32)
        pair_count = EXPERTS * CAPACITY
        pair_cell = jnp.arange(pair_count, dtype=jnp.int32) // CAPACITY
        own_hot = jax.random.randint(subkeys[2], (), 0, EXPERTS)
        cell_bias = jax.random.randint(subkeys[3], (EXPERTS,), 0, 4)
        cell_range = jnp.arange(EXPERTS, dtype=jnp.int32)
        cell_bias = jnp.where((cell_range == hot_all) | (cell_range == own_hot), 16, cell_bias).astype(jnp.int32)
        pair_score = cell_bias[pair_cell] * (pair_count // 4) + jax.random.permutation(subkeys[4], pair_count).astype(jnp.int32)
        chosen = pair_cell[jnp.argsort(-pair_score)[:LIVE_DEV]]
        chosen = chosen[jax.random.permutation(subkeys[5], LIVE_DEV)]
        position = jnp.arange(SAMPLES, dtype=jnp.int32)
        flat_live = (position[None, :] < lengths[:, None]).reshape(RAY_DEV * SAMPLES)
        rank_live = jnp.cumsum(flat_live.astype(jnp.int32)) - 1
        dead_cell = jax.random.randint(subkeys[6], (RAY_DEV * SAMPLES,), 0, EXPERTS)
        cell_ids = jnp.where(flat_live, chosen[jnp.clip(rank_live, 0, LIVE_DEV - 1)], dead_cell).astype(jnp.int32)
        onehot = (cell_ids[:, None] == cell_range[None, :]) & flat_live[:, None]
        counts = jnp.cumsum(onehot.astype(jnp.int32), axis=0) - 1
        slot_ranks = jnp.where(flat_live, jnp.take_along_axis(counts, cell_ids[:, None], axis=1)[:, 0], -1).astype(jnp.int32)
        return (lengths, cell_ids.reshape(RAY_DEV, SAMPLES), slot_ranks.reshape(RAY_DEV, SAMPLES))
    lengths, cell_ids, slot_ranks = lax.map(one_block, jnp.arange(blocks, dtype=jnp.int32))
    return (lengths.reshape(RAY_TOTAL), cell_ids.reshape(RAY_TOTAL, SAMPLES), slot_ranks.reshape(RAY_TOTAL, SAMPLES))


def draw_ray_length(key, part):
    return sample_layout(jax.random.fold_in(key, 5))[0]


def draw_cell_id(key, part):
    return sample_layout(jax.random.fold_in(key, 5))[1]


def draw_slot_rank(key, part):
    return sample_layout(jax.random.fold_in(key, 5))[2]


def draw_image_id(key, part):
    blocks = RAY_TOTAL // RAY_DEV
    local_ids = jax.random.randint(key, (blocks, RAY_DEV), 0, IMG_DEV)
    marked = jax.random.randint(jax.random.fold_in(key, 3), (blocks, 2), 0, RAY_DEV)
    row_number = jnp.arange(blocks, dtype=jnp.int32)
    local_ids = local_ids.at[row_number, marked[:, 1]].set(0)
    local_ids = local_ids.at[row_number, marked[:, 0]].set(IMG_DEV - 1)
    global_ids = local_ids + (row_number * IMG_DEV)[:, None]
    return global_ids.reshape(RAY_TOTAL).astype(jnp.int32)


def draw_params(key, part):
    head_row = ENC_WIDTH + (LAYERS - 1) * NET_WIDTH
    row_number = jnp.arange(PARAM_ROWS)
    row_scale = jnp.where(row_number < ENC_WIDTH, (2.0 / ENC_WIDTH) ** 0.5, (2.0 / NET_WIDTH) ** 0.5)
    row_scale = jnp.where(row_number >= head_row, NET_WIDTH ** (-0.5), row_scale)
    row_scale = jnp.where(row_number >= head_row + 4, 4.0 * CODE_WIDTH ** (-0.5), row_scale)
    row_scale = jnp.where(row_number >= head_row + 8, 0.3, row_scale)
    normals = jnp.clip(jax.random.normal(key, (EXPERTS, PARAM_ROWS, NET_WIDTH), jnp.float32), -5.0, 5.0)
    return normals * row_scale[None, :, None].astype(jnp.float32)


def levels(rng, shape, cuts, least, top_value):
    gain = 1.0
    for dim, parts in cuts:
        heights = jax.random.uniform(jax.random.fold_in(jax.random.fold_in(rng, 6), dim), (parts,), jnp.float32, least / len(cuts), top_value / len(cuts))
        gain = gain * jnp.repeat(jnp.exp(heights), shape[dim] // parts).reshape((-1,) + (1,) * (len(shape) - 1 - dim))
    return gain


def normal_values(stream_key, dims, deviation, limit, shards=(), kind=jnp.bfloat16):
    level = levels(stream_key, dims, shards, -0.22, 0.18) if shards else 1.0
    values = jax.random.normal(stream_key, dims, jnp.float32) * deviation * level
    return jnp.minimum(jnp.maximum(values, -limit), limit).astype(kind)


def setup_inputs(seed: int = 0) -> dict:
    key_list = jax.random.split(jax.random.key(seed), 14)
    return {
        "features": jnp.clip(jax.random.uniform(key_list[0], (RAY_TOTAL, SAMPLES, ENC_WIDTH), jnp.float32, -1.0, 1.0) * levels(key_list[0], (RAY_TOTAL, SAMPLES, ENC_WIDTH), ((0, 32),), -0.4, 0.0), -1.0, 1.0).astype(jnp.bfloat16),
        "spacing": jnp.clip(jnp.exp(math.log(0.3) - 2.7080503 * jax.random.uniform(key_list[1], (RAY_TOTAL, SAMPLES), jnp.float32) ** levels(key_list[1], (RAY_TOTAL, SAMPLES), ((0, 32),), -0.2, 0.2)), 0.02, 0.3),
        "targets": jnp.clip(1.0 * jax.random.uniform(key_list[2], (3, RAY_TOTAL), jnp.float32) ** levels(key_list[2], (3, RAY_TOTAL), ((1, 32),), -0.2, 0.2), 0.0, 1.0),
        "ray_length": draw_ray_length(jax.random.fold_in(key_list[13], 71), 0),
        "cell_id": draw_cell_id(jax.random.fold_in(key_list[13], 71), 0),
        "slot_rank": draw_slot_rank(jax.random.fold_in(key_list[13], 71), 0),
        "image_id": draw_image_id(jax.random.fold_in(key_list[13], 71), 0),
        "params": draw_params(jax.random.fold_in(key_list[13], 71), 0),
        "first_moment": normal_values(key_list[8], (EXPERTS, PARAM_ROWS, NET_WIDTH), 0.05, 0.75, ((0, 8),), jnp.float32),
        "second_moment": jnp.clip(jnp.exp(math.log(0.01) - 9.2103404 * jax.random.uniform(key_list[9], (EXPERTS, PARAM_ROWS, NET_WIDTH), jnp.float32) ** levels(key_list[9], (EXPERTS, PARAM_ROWS, NET_WIDTH), ((0, 8),), -0.2, 0.2)), 9.999999974752427e-07, 0.01),
        "code_table": normal_values(key_list[10], (IMAGES, CODE_WIDTH), 0.5, 6.0, ((0, 32),), jnp.float32),
        "table_first": normal_values(key_list[11], (IMAGES, CODE_WIDTH), 0.05, 0.75, ((0, 32),), jnp.float32),
        "table_second": jnp.clip(jnp.exp(math.log(0.01) - 9.2103404 * jax.random.uniform(key_list[12], (IMAGES, CODE_WIDTH), jnp.float32) ** levels(key_list[12], (IMAGES, CODE_WIDTH), ((0, 32),), -0.2, 0.2)), 9.999999974752427e-07, 0.01),
    }


BETA_ONE = 0.9
BETA_TWO = 0.999
LEARN_RATE = 0.001
ADAM_EPS = 1e-08
CORRECT_ONE = 1.0 - 0.9 ** 10
CORRECT_TWO = 1.0 - 0.999 ** 10

def adam_update(param_now, gradient, moment_one, moment_two):
    new_one = BETA_ONE * moment_one + (1.0 - BETA_ONE) * gradient
    new_two = BETA_TWO * moment_two + (1.0 - BETA_TWO) * gradient * gradient
    update = LEARN_RATE * (new_one / CORRECT_ONE) / (jnp.sqrt(new_two / CORRECT_TWO) + ADAM_EPS)
    return (param_now - update, new_one, new_two)

def composite(raw_out, spacing, live_mask, targets):
    density = jax.nn.softplus(raw_out[0])
    colors = jax.nn.sigmoid(raw_out[1:4])
    optical = density * spacing * live_mask
    before = jnp.cumsum(optical, axis=1) - optical
    weight = jnp.exp(-before) * (1.0 - jnp.exp(-optical))
    render = lax.optimization_barrier(jnp.sum(weight[None] * colors, axis=2))
    return 0.5 * lax.optimization_barrier(jnp.sum((render - targets) ** 2, axis=0))

def contract_first(left, right):
    return lax.dot_general(left.astype(jnp.float32), right.astype(jnp.float32), (((0,), (0,)), ((), ())))

def contract_last(left, right):
    return lax.dot_general(left.astype(jnp.float32), right.astype(jnp.float32), (((1,), (1,)), ((), ())))

def expert_forward(weights, inputs, code_rows):
    head_row = ENC_WIDTH + (LAYERS - 1) * NET_WIDTH
    activations = [inputs]
    preacts = []
    current = inputs
    row_start = 0
    row_count = ENC_WIDTH
    for layer_index in range(LAYERS):
        matrix = weights[row_start:row_start + row_count]
        preact = jnp.dot(current.astype(jnp.float32), matrix.astype(jnp.float32)) + weights[head_row + 9 + layer_index].astype(jnp.float32)
        current = jnp.maximum(preact, 0.0).astype(jnp.bfloat16)
        preacts.append(preact)
        activations.append(current)
        row_start = row_start + row_count
        row_count = NET_WIDTH
    hidden_part = contract_last(current, weights[head_row:head_row + 4])
    code_part = contract_last(code_rows, weights[head_row + 4:head_row + 8, :CODE_WIDTH])
    raw_out = hidden_part + code_part + weights[head_row + 8, :4].astype(jnp.float32)
    return (activations, preacts, raw_out)

def expert_backward(weights, activations, preacts, code_rows, cotangent):
    head_row = ENC_WIDTH + (LAYERS - 1) * NET_WIDTH
    hidden_head = contract_first(cotangent, activations[-1])
    code_head = contract_first(cotangent, code_rows)
    bias_head = lax.optimization_barrier(jnp.sum(cotangent.astype(jnp.float32), axis=0))
    code_grad = jnp.dot(cotangent.astype(jnp.float32), weights[head_row + 4:head_row + 8, :CODE_WIDTH].astype(jnp.float32))
    upstream = jnp.dot(cotangent.astype(jnp.float32), weights[head_row:head_row + 4].astype(jnp.float32))
    weight_grads = [None] * LAYERS
    bias_grads = [None] * LAYERS
    for layer_index in reversed(range(LAYERS)):
        pre_grad = jnp.where(preacts[layer_index] > 0, upstream, 0.0).astype(jnp.bfloat16)
        weight_grads[layer_index] = contract_first(activations[layer_index], pre_grad)
        bias_grads[layer_index] = lax.optimization_barrier(jnp.sum(pre_grad.astype(jnp.float32), axis=0))
        if layer_index > 0:
            row_start = ENC_WIDTH + (layer_index - 1) * NET_WIDTH
            upstream = contract_last(pre_grad, weights[row_start:row_start + NET_WIDTH])
    pieces = list(weight_grads) + [hidden_head, jnp.pad(code_head, ((0, 0), (0, NET_WIDTH - CODE_WIDTH))), jnp.pad(bias_head, (0, NET_WIDTH - 4))[None, :], jnp.stack(bias_grads, axis=0), jnp.zeros((7 - LAYERS, NET_WIDTH), jnp.float32)]
    return (jnp.concatenate(pieces, axis=0), code_grad)

def reference(features, spacing, targets, ray_length, cell_id, slot_rank, image_id, params, first_moment, second_moment, code_table, table_first, table_second):
    ray_total = features.shape[0]
    sample_count = ray_total * SAMPLES
    blocks = ray_total // RAY_DEV
    column_count = blocks * CAPACITY
    positions = features.reshape(sample_count, ENC_WIDTH)
    ray_code = code_table.astype(jnp.bfloat16)[image_id]
    sample_code = jnp.broadcast_to(ray_code[:, None, :], (ray_total, SAMPLES, CODE_WIDTH)).reshape(sample_count, CODE_WIDTH)
    flat_rank = slot_rank.reshape(sample_count)
    flat_cell = cell_id.reshape(sample_count)
    sample_numbers = jnp.arange(sample_count, dtype=jnp.int32)
    block_number = sample_numbers // (RAY_DEV * SAMPLES)
    column = jnp.where(flat_rank >= 0, block_number * CAPACITY + flat_rank, column_count).astype(jnp.int32)
    owner_ids = jnp.full((EXPERTS, column_count), -1, jnp.int32).at[flat_cell, column].set(sample_numbers, mode='drop')
    weights_bf = params.astype(jnp.bfloat16)

    def gather_rows(sample_ids):
        occupied = sample_ids >= 0
        safe_ids = jnp.maximum(sample_ids, 0)
        inputs = jnp.where(occupied[:, None], positions[safe_ids], jnp.zeros((), jnp.bfloat16))
        code_rows = jnp.where(occupied[:, None], sample_code[safe_ids], jnp.zeros((), jnp.bfloat16))
        return (occupied, safe_ids, inputs, code_rows)

    def forward_one(operands):
        weights, sample_ids = operands
        occupied, safe_ids, inputs, code_rows = gather_rows(sample_ids)
        return expert_forward(weights, inputs, code_rows)[2]
    raw_table = lax.map(forward_one, (weights_bf, owner_ids))
    live_flat = flat_rank >= 0
    raw_samples = raw_table[flat_cell, jnp.minimum(column, column_count - 1)]
    raw_samples = jnp.where(live_flat[:, None], raw_samples, 0.0)
    position = jnp.arange(SAMPLES, dtype=jnp.int32)
    live_mask = (position[None, :] < ray_length[:, None]).astype(jnp.float32)
    raw_grid = raw_samples.T.reshape(4, ray_total, SAMPLES)

    def loss_of(raw_in):
        return composite(raw_in, spacing, live_mask, targets)
    ray_loss, pullback = jax.vjp(loss_of, raw_grid)
    raw_grad, = pullback(jnp.ones_like(ray_loss))
    cotangent = raw_grad.reshape(4, sample_count).T.astype(jnp.bfloat16)

    def backward_one(code_sum, operands):
        weights, sample_ids = operands
        occupied, safe_ids, inputs, code_rows = gather_rows(sample_ids)
        upstream_rows = jnp.where(occupied[:, None], cotangent[safe_ids], jnp.zeros((), jnp.bfloat16))
        activations, preacts, raw_out = expert_forward(weights, inputs, code_rows)
        gradient, code_grad = expert_backward(weights, activations, preacts, code_rows, upstream_rows)
        code_sum = code_sum.at[safe_ids // SAMPLES].add(jnp.where(occupied[:, None], code_grad, 0.0))
        return (code_sum, gradient)
    ray_code_grad, param_grad = lax.scan(backward_one, jnp.zeros((ray_total, CODE_WIDTH), jnp.float32), (weights_bf, owner_ids))
    table_grad = jax.ops.segment_sum(ray_code_grad, image_id, num_segments=IMAGES)
    new_params, new_first, new_second = adam_update(params, param_grad, first_moment, second_moment)
    new_table, new_table_first, new_table_second = adam_update(code_table, table_grad, table_first, table_second)
    return (ray_loss, new_params, new_first, new_second, new_table, new_table_first, new_table_second)
```

```python
import functools

import jax
import jax.numpy as jnp
from jax import lax
from jax.experimental import pallas as pl
from jax.experimental.pallas import tpu as pltpu
from jax.sharding import PartitionSpec as P

NET_WIDTH = 256
CODE_WIDTH = 64
ENC_WIDTH = 64
LAYERS = 4
SAMPLES = 32
HEAD_ROW = ENC_WIDTH + (LAYERS - 1) * NET_WIDTH
LANES = 128

BETA_ONE = 0.9
BETA_TWO = 0.999
LEARN_RATE = 0.001
ADAM_EPS = 1e-08
CORRECT_ONE = 1.0 - 0.9**10
CORRECT_TWO = 1.0 - 0.999**10

MESH = pl.DeviceIdType.MESH
VMEM = pl.BlockSpec(memory_space=pltpu.VMEM)
HBM = pl.BlockSpec(memory_space=pltpu.HBM)
F32 = jnp.float32
BF16 = jnp.bfloat16
NN = (((1,), (0,)), ((), ()))
NT = (((1,), (1,)), ((), ()))
TN = (((0,), (0,)), ((), ()))


def dot(left, right, dims=NN, precision=None):
    return lax.dot_general(left, right, dims, precision=precision, preferred_element_type=F32)


def exact(left, right, dims=NN):
    return dot(left, right, dims, lax.Precision.HIGHEST)


def adam_update(param_now, gradient, moment_one, moment_two):
    new_one = BETA_ONE * moment_one + (1.0 - BETA_ONE) * gradient
    new_two = BETA_TWO * moment_two + (1.0 - BETA_TWO) * gradient * gradient
    update = LEARN_RATE * (new_one / CORRECT_ONE) / (jnp.sqrt(new_two / CORRECT_TWO) + ADAM_EPS)
    return (param_now - update, new_one, new_two)


def iota(shape, dim):
    return lax.broadcasted_iota(jnp.int32, shape, dim)


def lane_block(index):
    return pl.ds(pl.multiple_of(index * LANES, LANES), LANES)


def rows_of(index, count, align=8):
    return pl.ds(pl.multiple_of(index * count, align), count)


def place_kernel(
    groups, cap, cap_up, cell_ref, rank_ref, feat_hbm, out_ref,
    feat, rows, table, counts, slot_vec, slot, feat_sem, slot_sem,
):
    load = pltpu.make_async_copy(feat_hbm, feat, feat_sem)
    load.start()
    cell = cell_ref[...]
    rank = rank_ref[...]
    live = rank >= 0
    slot_vec[...] = jnp.where(live, cell * cap_up + rank, 2 * groups * cap_up)
    scalars = pltpu.make_async_copy(slot_vec, slot, slot_sem)
    scalars.start()
    kind = jnp.where(live, cell, -1)

    def count(g, carry):
        parts = [
            jnp.sum(jnp.where(kind == 8 * g + j, 1.0, 0.0), axis=0, keepdims=True)
            for j in range(8)
        ]
        total = jnp.sum(jnp.concatenate(parts, axis=0), axis=1, keepdims=True)
        counts[rows_of(g, 8), :] = jnp.broadcast_to(total, (8, LANES))
        return carry

    lax.fori_loop(0, 2 * groups // 8, count, 0)
    load.wait()

    def turn(index, carry):
        for inner in range(4):
            i = index * 4 + inner
            block = feat[i].astype(F32)
            rows[lane_block(i), :] = jnp.concatenate([block, block], axis=0).T
        return carry

    lax.fori_loop(0, SAMPLES // 4, turn, 0)
    scalars.wait()
    for i in range(SAMPLES):

        def move(r, carry):
            table[pl.ds(slot[i, r], 1), :] = rows[pl.ds(i * LANES + r, 1), :]
            return carry

        lax.fori_loop(0, LANES, move, 0, unroll=True)
    low = iota((1, LANES), 1) < ENC_WIDTH
    position = iota((cap, LANES), 0).astype(F32)

    def pack(g, carry):
        first = table[pl.ds(pl.multiple_of(2 * g * cap_up, LANES), cap), :]
        second = table[pl.ds(pl.multiple_of((2 * g + 1) * cap_up, LANES), cap), :]
        limit = jnp.where(low, counts[pl.ds(2 * g, 1), :], counts[pl.ds(2 * g + 1, 1), :])
        value = jnp.where(low, first, second)
        out_ref[g] = jnp.where(position < limit, value, 0.0).astype(BF16)
        return carry

    lax.fori_loop(0, groups, pack, 0)


def flipped(me, k, groups):
    peer = 0
    bit = 1
    while bit < groups:
        peer = peer + bit * lax.rem(lax.div(me, bit) + lax.div(k, bit), 2)
        bit *= 2
    return peer


def layer_matrix(wt, m0, h, layer):
    if layer == 0:
        return m0[h]
    start = ENC_WIDTH + (layer - 1) * NET_WIDTH
    return wt[h, start : start + NET_WIDTH, :]


def tail_rows(wt, h):
    return wt[h, HEAD_ROW : HEAD_ROW + 16, :]


def prefix(value, row, backwards):
    step = 1
    while step < SAMPLES:
        if backwards:
            moved = jnp.where(row < SAMPLES - step, pltpu.roll(value, SAMPLES - step, 0), 0.0)
        else:
            moved = jnp.where(row >= step, pltpu.roll(value, step, 0), 0.0)
        value = value + moved
        step *= 2
    return value


def step_kernel(
    groups, cap, cap_up,
    disp, params, cell_ref, rank_ref, spacing_ref, length_ref, target_ref, image_ref,
    code_ref, first_ref, second_ref,
    grad_out, loss_out, code_out, first_out, second_out,
    master, tails_f32, wt, m0, turned, head, recv, act, pre,
    raw_msg, back, tail_msg, tails, queries, shift, mix, eight, keys, wide, spots,
    cot_msg, cot_in, code_msg, code_in, cot_sum, bias, grad, half_in, sum_out, sum_in, full,
    load_sems, s_out, r_out, s_back, r_back, s_tail, r_tail, s_cot, r_cot, s_code, r_code,
    s_sum, r_sum,
):
    tiles = cap_up // LANES
    half = max(groups // 2 - 1, 0)
    me = lax.axis_index("expert")
    my_dp = lax.axis_index("dp")
    core = lax.rem(my_dp, 2)
    near = my_dp + 1 - 2 * core
    far = my_dp + 2 - 4 * lax.rem(lax.div(my_dp, 2), 2)
    load_tail = pltpu.make_async_copy(
        params.at[:, HEAD_ROW : HEAD_ROW + 16, :], tails_f32, load_sems.at[0]
    )
    load_tail.start()
    load = pltpu.make_async_copy(params, master, load_sems.at[1])
    load.start()

    barrier = pltpu.get_barrier_semaphore()

    def greet(k, carry):
        pl.semaphore_signal(
            barrier, 1, device_id={"expert": lax.rem(me + k, groups)}, device_id_type=MESH
        )
        return carry

    lax.fori_loop(1, groups, greet, 0)
    for peer in (near, far):
        pl.semaphore_signal(barrier, 1, device_id={"dp": peer}, device_id_type=MESH)

    def turn_of(j):
        return lax.rem(j - 1 + half, groups - 1) + 1

    def block_rows(k):
        return rows_of(k, cap, 16)

    def peer_copy(k, source, target, sends, receives):
        return pltpu.make_async_remote_copy(
            source, target, sends.at[k], receives.at[k],
            device_id={"expert": flipped(me, k, groups)}, device_id_type=MESH,
        )

    def out_copy(k):
        return peer_copy(k, disp.at[flipped(me, k, groups)], recv.at[block_rows(k)], s_out, r_out)

    def back_copy(k):
        return peer_copy(k, raw_msg.at[k], back.at[me], s_back, r_back)

    def tail_copy(k):
        return peer_copy(k, tail_msg, tails.at[me], s_tail, r_tail)

    def cot_copy(k):
        return peer_copy(k, cot_msg.at[flipped(me, k, groups)], cot_in.at[k], s_cot, r_cot)

    def code_copy(k):
        return peer_copy(k, code_msg.at[flipped(me, k, groups)], code_in.at[k], s_code, r_code)

    def each(body):
        def turn(j, carry):
            body(turn_of(j))
            return carry

        lax.fori_loop(1, groups, turn, 0)

    load_tail.wait()
    spot = iota((4, LANES), 0) == iota((4, LANES), 1)
    lane = iota((4, LANES), 1)
    for h in range(2):
        tail = tails_f32[h].astype(BF16).astype(F32)
        column = jnp.sum(jnp.where(spot, tail[8:9, 0:LANES], 0.0), axis=1, keepdims=True)
        tail_msg[4 * h : 4 * h + 4, :] = jnp.where(
            lane < CODE_WIDTH, tail[4:8, 0:LANES], jnp.where(lane == CODE_WIDTH, column, 0.0)
        )
    tails[me] = tail_msg[...]
    pl.semaphore_wait(barrier, groups + 1)
    each(lambda k: tail_copy(k).start())
    each(lambda k: out_copy(k).start())

    load.wait()
    wt[...] = master[...].astype(BF16)
    m0[...] = jnp.zeros_like(m0)
    head[...] = jnp.zeros_like(head)
    for h in range(2):
        m0[h, ENC_WIDTH * h : ENC_WIDTH * (h + 1), :] = wt[h, 0:ENC_WIDTH, :]
        head[h, 4 * h : 4 * h + 4, :] = tail_rows(wt, h).astype(F32)[0:4]
    recv[block_rows(0), :] = disp[me]

    def process(k):
        block = block_rows(k)
        features = recv[block, :]
        biases = [tail_rows(wt, h).astype(F32) for h in range(2)]
        current = [features, features]
        for layer in range(LAYERS):
            for h in range(2):
                preact = dot(current[h], layer_matrix(wt, m0, h, layer))
                preact = preact + biases[h][9 + layer : 10 + layer, :]
                current[h] = jnp.maximum(preact, 0.0).astype(BF16)
                act[layer, h, block, :] = current[h]
        for h in range(2):
            raw = dot(tail_rows(wt, h), current[h], NT)
            raw_msg[k, 4 * h : 4 * h + 4, 0:cap] = raw[0:4]

    process(0)
    back[me] = raw_msg[0]

    for h in range(2):
        for layer in range(1, LAYERS):
            matrix = layer_matrix(wt, m0, h, layer)
            turned[layer - 1, h] = matrix.astype(F32).T.astype(BF16)

    cell = cell_ref[...]
    rank = rank_ref[...]
    row = iota((SAMPLES, LANES), 0)
    live = row < length_ref[...]
    place = jnp.where(live, rank, 0)
    tile = lax.div(place, LANES)
    lane_index = place - tile * LANES
    key = jnp.where(live, cell * tiles + tile, -1)
    table_rows = code_ref.shape[0]
    block_index = me * lax.axis_size("dp") + my_dp
    pick = (
        iota((table_rows, LANES), 0) == image_ref[...] - block_index * table_rows
    ).astype(F32)
    ray_code = exact(code_ref[...].astype(BF16).astype(F32), pick, TN)

    keys[...] = key.astype(F32)
    eight[0:SAMPLES, :] = lane_index.astype(F32)
    slot_lane = iota((LANES, LANES), 0).astype(F32)

    def spread(i, carry):
        line = jnp.broadcast_to(eight[pl.ds(i, 1), :], (LANES, LANES))
        spots[:, lane_block(i)] = jnp.where(line == slot_lane, 1.0, 0.0).astype(BF16)
        return carry

    lax.fori_loop(0, SAMPLES, spread, 0)

    def step(j, carry):
        k = turn_of(j)
        out_copy(k).wait_recv()
        process(k)
        back_copy(k).start()
        return carry

    lax.fori_loop(1, groups, step, 0)

    each(lambda k: tail_copy(k).wait_recv())

    def collect(g, carry):
        queries[rows_of(g, 8), :] = tails[g, :, 0:CODE_WIDTH]
        shift[rows_of(g, 8), :] = jnp.broadcast_to(
            tails[g, :, CODE_WIDTH : CODE_WIDTH + 1], (8, LANES)
        )
        return carry

    lax.fori_loop(0, groups, collect, 0)
    mix[...] = exact(queries[...], ray_code) + shift[...]
    zero = jnp.zeros((SAMPLES, LANES), F32)

    def add_code(g, codes):
        part = mix[rows_of(g, 8), :]
        codes = list(codes)
        for h in range(2):
            hit = cell == 2 * g + h
            for c in range(4):
                j = 4 * h + c
                codes[c] = jnp.where(hit, part[j : j + 1, :], codes[c])
        return tuple(codes)

    codes = lax.fori_loop(0, groups, add_code, (zero,) * 4)

    def take(g, raws):
        raws = list(raws)
        for t in range(tiles):
            piece = back[g, :, t * LANES : (t + 1) * LANES]
            for h in range(2):
                hit = key == (2 * g + h) * tiles + t
                for c in range(4):
                    j = 4 * h + c
                    line = jnp.broadcast_to(piece[j : j + 1, :], (SAMPLES, LANES))
                    found = jnp.take_along_axis(line, lane_index, axis=1)
                    raws[c] = jnp.where(hit, found, raws[c])
        return tuple(raws)

    raws = take(me, (zero,) * 4)

    def take_next(j, raws):
        k = turn_of(j)
        back_copy(k).wait_recv()
        return take(flipped(me, k, groups), raws)

    raws = lax.fori_loop(1, groups, take_next, raws)
    raws = [jnp.where(live, raws[c] + codes[c], 0.0) for c in range(4)]
    spacing = spacing_ref[...]
    density = jnp.maximum(raws[0], 0.0) + jnp.log1p(jnp.exp(-jnp.abs(raws[0])))
    colors = [jax.nn.sigmoid(raw) for raw in raws[1:]]
    tau = jnp.where(live, density * spacing, 0.0)
    before = prefix(tau, row, False) - tau
    through = jnp.exp(-before)
    fade = jnp.exp(-tau)
    weight = through * (1.0 - fade)
    gaps = [
        jnp.sum(weight * colors[c], axis=0, keepdims=True) - target_ref[c : c + 1, :]
        for c in range(3)
    ]
    loss_out[...] = 0.5 * (gaps[0] * gaps[0] + gaps[1] * gaps[1] + gaps[2] * gaps[2])
    pull = gaps[0] * colors[0] + gaps[1] * colors[1] + gaps[2] * colors[2]
    gain = pull * weight
    after = prefix(gain, row, True) - gain
    tau_grad = pull * through * fade - after
    grads = [tau_grad * spacing * jax.nn.sigmoid(raws[0])]
    for c in range(3):
        grads.append(gaps[c] * weight * colors[c] * (1.0 - colors[c]))
    for c in range(4):
        cot = jnp.where(live, grads[c], 0.0).astype(BF16).astype(F32)
        eight[pl.ds(c, SAMPLES, 8), :] = cot
        eight[pl.ds(4 + c, SAMPLES, 8), :] = cot
    mix[...] = jnp.zeros_like(mix)
    member = lax.div(iota((8, LANES), 0), 4) * tiles

    def widen(i, carry):
        value = eight[rows_of(i, 8), :]
        line = jnp.broadcast_to(keys[pl.ds(i, 1), :], (8, LANES))
        sums = [0.0] * groups
        for t in range(tiles):
            for pair in range(groups // 2):
                both = []
                for g in (2 * pair, 2 * pair + 1):
                    want = (member + (2 * g * tiles + t)).astype(F32)
                    chosen = jnp.where(line == want, value, 0.0)
                    sums[g] = sums[g] + chosen
                    both.append(chosen)
                start = (t * groups + 2 * pair) * 8
                wide[start : start + 16, lane_block(i)] = jnp.concatenate(both, axis=0).astype(BF16)
        for g in range(groups):
            mix[8 * g : 8 * g + 8, :] += sums[g]
        return carry

    lax.fori_loop(0, SAMPLES, widen, 0)
    slots = dot(wide[...], spots[...], NT)
    for t in range(tiles):
        for g in range(groups):
            start = (t * groups + g) * 8
            cot_msg[g, :, t * LANES : (t + 1) * LANES] = slots[start : start + 8].astype(BF16)
    each(lambda k: cot_copy(k).start())
    cot_in[0] = cot_msg[me]

    totals = mix[...]
    query_grad = exact(totals, ray_code, NT)
    for g in range(groups):
        code_msg[g, :, 0:CODE_WIDTH] = query_grad[8 * g : 8 * g + 8]
        code_msg[g, :, CODE_WIDTH:] = jnp.zeros((8, LANES - CODE_WIDTH), F32)
    each(lambda k: code_copy(k).start())
    code_in[0] = code_msg[me]
    table_grad = exact(exact(totals, pick, NT), queries[...], TN)
    new_code, new_first, new_second = adam_update(
        code_ref[...], table_grad, first_ref[...], second_ref[...]
    )
    code_out[...] = new_code
    first_out[...] = new_first
    second_out[...] = new_second

    starts = [0] + [ENC_WIDTH + layer * NET_WIDTH for layer in range(LAYERS)] + [HEAD_ROW + 16]
    chunks = [pl.ds(starts[j], starts[j + 1] - starts[j]) for j in range(LAYERS + 1)]

    def near_copy(j):
        return pltpu.make_async_remote_copy(
            grad.at[1 - core, chunks[j]], half_in.at[chunks[j]],
            s_sum.at[0, j], r_sum.at[0, j], device_id={"dp": near}, device_id_type=MESH,
        )

    def far_copy(j):
        return pltpu.make_async_remote_copy(
            sum_out.at[chunks[j]], sum_in.at[chunks[j]],
            s_sum.at[1, j], r_sum.at[1, j], device_id={"dp": far}, device_id_type=MESH,
        )

    def full_copy(j, which):
        return pltpu.make_async_remote_copy(
            full.at[which, chunks[j]], full.at[which, chunks[j]],
            s_sum.at[2, j], r_sum.at[2, j], device_id={"dp": near}, device_id_type=MESH,
        )

    def second_stage(j):
        near_copy(j).wait_recv()
        rows = chunks[j]
        sum_out[rows, :] = (grad[core, rows, :] + half_in[rows, :]).astype(BF16)
        far_copy(j).start()

    def third_stage(j):
        far_copy(j).wait_recv()
        rows = chunks[j]
        full[core, rows, :] = sum_out[rows, :].astype(F32) + sum_in[rows, :].astype(F32)
        full_copy(j, core).start()

    top = LAYERS - 1
    heads_bf = [head[h].astype(BF16) for h in range(2)]
    bias[...] = jnp.zeros_like(bias)
    cot_sum[...] = jnp.zeros_like(cot_sum)

    def mask_store(layer, h, block, up):
        value = jnp.where(act[layer, h, block, :].astype(F32) > 0, up, 0.0).astype(BF16)
        pre[layer, h, block, :] = value
        bias[layer, h] += jnp.sum(value.astype(F32).reshape(-1, 8, NET_WIDTH), axis=0)

    def first_back(k, carry):
        block = block_rows(k)
        cot = cot_in[k, :, 0:cap]
        sums = []
        for h in range(2):
            mask_store(top, h, block, dot(cot, heads_bf[h], TN))
            sums.append(carry[h] + dot(cot, act[top, h, block, :]))
        cot_sum[...] += jnp.broadcast_to(
            jnp.sum(cot.astype(F32), axis=1, keepdims=True), (8, LANES)
        )
        return tuple(sums)

    def next_back(j, carry):
        k = turn_of(j)
        cot_copy(k).wait_recv()
        return first_back(k, carry)

    zeros = jnp.zeros((8, NET_WIDTH), F32)
    hidden = lax.fori_loop(1, groups, next_back, first_back(0, (zeros, zeros)))

    pieces = 4
    size = recv.shape[0] // pieces
    for layer in reversed(range(LAYERS)):
        if layer < top:

            def onward(index, carry):
                block = rows_of(index, size, 16)
                for h in range(2):
                    mask_store(
                        layer, h, block, dot(pre[layer + 1, h, block, :], turned[layer, h])
                    )
                return carry

            lax.fori_loop(0, pieces, onward, 0)
        for h in range(2):
            if layer == 0:
                value = dot(recv[...], pre[0, h], TN)
                grad[h, 0:ENC_WIDTH, :] = value[ENC_WIDTH * h : ENC_WIDTH * (h + 1)]
            else:
                grad[h, chunks[layer], :] = dot(act[layer - 1, h], pre[layer, h], TN)
        near_copy(layer).start()
        if layer < top:
            second_stage(layer + 1)
        if layer < top - 1:
            third_stage(layer + 2)

    def add_codes(k, carry):
        code_copy(k).wait_recv()
        return carry + code_in[k]

    code_sum = lax.fori_loop(1, groups, add_codes, code_in[0])
    codes = jnp.concatenate([code_sum, jnp.zeros((8, NET_WIDTH - LANES), F32)], axis=1)
    spot = iota((8, LANES), 0) == iota((8, LANES), 1)
    cot_row = jnp.sum(jnp.where(spot, cot_sum[...], 0.0), axis=0, keepdims=True)
    lane = iota((1, LANES), 1)
    for h in range(2):
        line = cot_row if h == 0 else pltpu.roll(cot_row, LANES - 4, 1)
        line = jnp.where(lane < 4, line, 0.0)
        line = jnp.concatenate([line, jnp.zeros((1, NET_WIDTH - LANES), F32)], axis=1)
        grad[h, HEAD_ROW : HEAD_ROW + 16, :] = jnp.concatenate(
            [hidden[h][4 * h : 4 * h + 4], codes[4 * h : 4 * h + 4], line]
            + [jnp.sum(bias[layer, h], axis=0, keepdims=True) for layer in range(LAYERS)]
            + [jnp.zeros((7 - LAYERS, NET_WIDTH), F32)],
            axis=0,
        )
    near_copy(LAYERS).start()
    second_stage(0)
    third_stage(1)
    second_stage(LAYERS)
    third_stage(0)
    third_stage(LAYERS)

    def drain(k):
        for copy in (tail_copy, out_copy, back_copy, cot_copy, code_copy):
            copy(k).wait_send()

    each(drain)
    for j in (3, 2, 1, 0, LAYERS):
        near_copy(j).wait_send()
        far_copy(j).wait_send()
        full_copy(j, core).wait_send()
        full_copy(j, 1 - core).wait_recv()
        grad_out[:, chunks[j], :] = full[:, chunks[j], :]


def shards(
    features, spacing, targets, ray_length, cell_id, slot_rank, image_id,
    params, first_moment, second_moment, code_table, table_first, table_second,
):
    ray_rows = features.shape[0]
    sample_count = ray_rows * SAMPLES
    groups = lax.axis_size("expert")
    experts_all = params.shape[0] * groups
    cap = 2 * (sample_count * 3 // 4 // experts_all)
    cap_up = -(-cap // LANES) * LANES
    tiles = cap_up // LANES
    slots_up = experts_all * cap_up
    shape = jax.ShapeDtypeStruct
    scratch = pltpu.VMEM
    sem = pltpu.SemaphoreType.DMA
    cell = cell_id.T
    rank = slot_rank.T
    disp = pl.pallas_call(
        functools.partial(place_kernel, groups, cap, cap_up),
        out_shape=shape((groups, cap, LANES), BF16),
        in_specs=[VMEM, VMEM, HBM],
        out_specs=VMEM,
        scratch_shapes=[
            scratch((SAMPLES, ENC_WIDTH, ray_rows), BF16),
            scratch((sample_count, LANES), F32),
            scratch((slots_up + 8, LANES), F32),
            scratch((experts_all, LANES), F32),
            scratch((SAMPLES, LANES), jnp.int32),
            pltpu.SMEM((SAMPLES, LANES), jnp.int32),
            sem, sem,
        ],
        compiler_params=pltpu.CompilerParams(vmem_limit_bytes=48 * 2**20),
        cost_estimate=pl.CostEstimate(flops=0, bytes_accessed=6000 * sample_count, transcendentals=0),
        name="place",
    )(cell, rank, features.transpose(1, 2, 0))
    all_rows = groups * cap
    grad_rows = params.shape[1]
    table_shape = shape(code_table.shape, F32)
    peers = sem((groups,))
    param_grad, loss, new_table, new_table_first, new_table_second = pl.pallas_call(
        functools.partial(step_kernel, groups, cap, cap_up),
        out_shape=(
            shape(params.shape, F32), shape((1, ray_rows), F32), table_shape, table_shape, table_shape,
        ),
        in_specs=[VMEM, HBM] + [VMEM] * 9,
        out_specs=(VMEM,) * 5,
        scratch_shapes=[
            scratch(params.shape, F32),
            scratch((2, 16, NET_WIDTH), F32),
            scratch(params.shape, BF16),
            scratch((2, LANES, NET_WIDTH), BF16),
            scratch((LAYERS - 1, 2, NET_WIDTH, NET_WIDTH), BF16),
            scratch((2, 8, NET_WIDTH), F32),
            scratch((all_rows, LANES), BF16),
            scratch((LAYERS, 2, all_rows, NET_WIDTH), BF16),
            scratch((LAYERS, 2, all_rows, NET_WIDTH), BF16),
            scratch((groups, 8, cap_up), F32),
            scratch((groups, 8, cap_up), F32),
            scratch((8, LANES), F32),
            scratch((groups, 8, LANES), F32),
            scratch((8 * groups, CODE_WIDTH), F32),
            scratch((8 * groups, LANES), F32),
            scratch((8 * groups, LANES), F32),
            scratch((8 * SAMPLES, LANES), F32),
            scratch((SAMPLES, LANES), F32),
            scratch((tiles * groups * 8, sample_count), BF16),
            scratch((LANES, sample_count), BF16),
            scratch((groups, 8, cap_up), BF16),
            scratch((groups, 8, cap_up), BF16),
            scratch((groups, 8, LANES), F32),
            scratch((groups, 8, LANES), F32),
            scratch((8, LANES), F32),
            scratch((LAYERS, 2, 8, NET_WIDTH), F32),
            scratch((2, grad_rows, NET_WIDTH), F32),
            scratch((grad_rows, NET_WIDTH), F32),
            scratch((grad_rows, NET_WIDTH), BF16),
            scratch((grad_rows, NET_WIDTH), BF16),
            scratch((2, grad_rows, NET_WIDTH), F32),
            sem((2,)),
            peers, peers, peers, peers, peers, peers, peers, peers, peers, peers,
            sem((3, LAYERS + 1)),
            sem((3, LAYERS + 1)),
        ],
        compiler_params=pltpu.CompilerParams(
            collective_id=0, has_side_effects=True, vmem_limit_bytes=52 * 2**20
        ),
        cost_estimate=pl.CostEstimate(flops=0, bytes_accessed=50000 * sample_count, transcendentals=0),
        name="step",
    )(
        disp, params, cell, rank, spacing.T, ray_length[None, :], targets, image_id[None, :],
        code_table, table_first, table_second,
    )
    new_params, new_first, new_second = adam_update(params, param_grad, first_moment, second_moment)
    return (
        loss.reshape(ray_rows), new_params, new_first, new_second,
        new_table, new_table_first, new_table_second,
    )


def solution(mesh):
    both = ("expert", "dp")
    return jax.shard_map(
        shards,
        mesh=mesh,
        in_specs=(
            P(both, None, None), P(both, None), P(None, both), P(both), P(both, None),
            P(both, None), P(both),
            P("expert", None, None), P("expert", None, None), P("expert", None, None),
            P(both, None), P(both, None), P(both, None),
        ),
        out_specs=(
            P(both),
            P("expert", None, None), P("expert", None, None), P("expert", None, None),
            P(both, None), P(both, None), P(both, None),
        ),
        check_vma=False,
    )
```

```python
import functools

import jax
import jax.numpy as jnp
from jax import lax
from jax.experimental import pallas as pl
from jax.experimental.pallas import tpu as pltpu
from jax.sharding import PartitionSpec as P

NET_WIDTH = 256
CODE_WIDTH = 64
ENC_WIDTH = 64
LAYERS = 4
SAMPLES = 32
HEAD_ROW = ENC_WIDTH + (LAYERS - 1) * NET_WIDTH
LANES = 128

BETA_ONE = 0.9
BETA_TWO = 0.999
LEARN_RATE = 0.001
ADAM_EPS = 1e-08
CORRECT_ONE = 1.0 - 0.9**10
CORRECT_TWO = 1.0 - 0.999**10

MESH = pl.DeviceIdType.MESH
VMEM = pl.BlockSpec(memory_space=pltpu.VMEM)
HBM = pl.BlockSpec(memory_space=pltpu.HBM)
F32 = jnp.float32
BF16 = jnp.bfloat16
NN = (((1,), (0,)), ((), ()))
NT = (((1,), (1,)), ((), ()))
TN = (((0,), (0,)), ((), ()))


def dot(left, right, dims=NN, precision=None):
    return lax.dot_general(left, right, dims, precision=precision, preferred_element_type=F32)


def exact(left, right, dims=NN):
    return dot(left, right, dims, lax.Precision.HIGHEST)


def adam_update(param_now, gradient, moment_one, moment_two):
    new_one = BETA_ONE * moment_one + (1.0 - BETA_ONE) * gradient
    new_two = BETA_TWO * moment_two + (1.0 - BETA_TWO) * gradient * gradient
    update = LEARN_RATE * (new_one / CORRECT_ONE) / (jnp.sqrt(new_two / CORRECT_TWO) + ADAM_EPS)
    return (param_now - update, new_one, new_two)


def iota(shape, dim):
    return lax.broadcasted_iota(jnp.int32, shape, dim)


def lane_block(index):
    return pl.ds(pl.multiple_of(index * LANES, LANES), LANES)


def rows_of(index, count, align=8):
    return pl.ds(pl.multiple_of(index * count, align), count)


def place_kernel(
    groups, cap, cap_up, cell_hbm, rank_hbm, feat_hbm, params_hbm, *refs,
):
    smalls = refs[:7]
    out_ref, wt, cell_ref, rank_ref = refs[7:11]
    small_outs = refs[11:18]
    master, feat, rows, table, counts, slot_vec, slot, load_sems, slot_sem = refs[18:]
    pairs = [(cell_hbm, cell_ref), (rank_hbm, rank_ref), (feat_hbm, feat), (params_hbm, master)]
    pairs += list(zip(smalls, small_outs))
    loads = [
        pltpu.make_async_copy(source, target, load_sems.at[n])
        for n, (source, target) in enumerate(pairs)
    ]
    for load in loads:
        load.start()
    loads[0].wait()
    loads[1].wait()
    cell = cell_ref[...]
    rank = rank_ref[...]
    live = rank >= 0
    slot_vec[...] = jnp.where(live, cell * cap_up + rank, 2 * groups * cap_up)
    scalars = pltpu.make_async_copy(slot_vec, slot, slot_sem)
    scalars.start()
    kind = jnp.where(live, cell, -1)

    def count(g, carry):
        parts = [
            jnp.sum(jnp.where(kind == 8 * g + j, 1.0, 0.0), axis=0, keepdims=True)
            for j in range(8)
        ]
        total = jnp.sum(jnp.concatenate(parts, axis=0), axis=1, keepdims=True)
        counts[rows_of(g, 8), :] = jnp.broadcast_to(total, (8, LANES))
        return carry

    lax.fori_loop(0, 2 * groups // 8, count, 0)
    loads[2].wait()

    def turn(index, carry):
        for inner in range(4):
            i = index * 4 + inner
            block = feat[i].astype(F32)
            rows[lane_block(i), :] = jnp.concatenate([block, block], axis=0).T
        return carry

    lax.fori_loop(0, SAMPLES // 4, turn, 0)
    scalars.wait()
    for i in range(SAMPLES):

        def move(r, carry):
            table[pl.ds(slot[i, r], 1), :] = rows[pl.ds(i * LANES + r, 1), :]
            return carry

        lax.fori_loop(0, LANES, move, 0, unroll=True)
    low = iota((1, LANES), 1) < ENC_WIDTH
    position = iota((cap, LANES), 0).astype(F32)

    def pack(g, carry):
        first = table[pl.ds(pl.multiple_of(2 * g * cap_up, LANES), cap), :]
        second = table[pl.ds(pl.multiple_of((2 * g + 1) * cap_up, LANES), cap), :]
        limit = jnp.where(low, counts[pl.ds(2 * g, 1), :], counts[pl.ds(2 * g + 1, 1), :])
        value = jnp.where(low, first, second)
        out_ref[g] = jnp.where(position < limit, value, 0.0).astype(BF16)
        return carry

    lax.fori_loop(0, groups, pack, 0)
    for load in loads[3:]:
        load.wait()
    wt[...] = master[...].astype(BF16)


def flipped(me, k, groups):
    peer = 0
    bit = 1
    while bit < groups:
        peer = peer + bit * lax.rem(lax.div(me, bit) + lax.div(k, bit), 2)
        bit *= 2
    return peer


def layer_matrix(wt, m0, h, layer):
    if layer == 0:
        return m0[h]
    start = ENC_WIDTH + (layer - 1) * NET_WIDTH
    return wt[h, start : start + NET_WIDTH, :]


def tail_rows(wt, h):
    return wt[h, HEAD_ROW : HEAD_ROW + 16, :]


def prefix(value, row, backwards):
    step = 1
    while step < SAMPLES:
        if backwards:
            moved = jnp.where(row < SAMPLES - step, pltpu.roll(value, SAMPLES - step, 0), 0.0)
        else:
            moved = jnp.where(row >= step, pltpu.roll(value, step, 0), 0.0)
        value = value + moved
        step *= 2
    return value


def step_kernel(
    groups, cap, cap_up,
    disp, wt, cell_ref, rank_ref, spacing_ref, length_ref, target_ref, image_ref,
    code_ref, first_ref, second_ref,
    grad_out, loss_out, code_out, first_out, second_out,
    m0, turned, head, recv, act, pre,
    raw_msg, back, tail_msg, tails, queries, shift, mix, eight, keys, wide, spots,
    cot_msg, cot_in, code_msg, code_in, cot_sum, bias, grad, half_in, sum_out, sum_in, full,
    s_out, r_out, s_back, r_back, s_tail, r_tail, s_cot, r_cot, s_code, r_code,
    s_sum, r_sum,
):
    tiles = cap_up // LANES
    half = max(groups // 2 - 1, 0)
    me = lax.axis_index("expert")
    my_dp = lax.axis_index("dp")
    core = lax.rem(my_dp, 2)
    near = my_dp + 1 - 2 * core
    far = my_dp + 2 - 4 * lax.rem(lax.div(my_dp, 2), 2)
    barrier = pltpu.get_barrier_semaphore()

    def greet(k, carry):
        pl.semaphore_signal(
            barrier, 1, device_id={"expert": lax.rem(me + k, groups)}, device_id_type=MESH
        )
        return carry

    lax.fori_loop(1, groups, greet, 0)
    for peer in (near, far):
        pl.semaphore_signal(barrier, 1, device_id={"dp": peer}, device_id_type=MESH)

    def turn_of(j):
        return lax.rem(j - 1 + half, groups - 1) + 1

    def block_rows(k):
        return rows_of(k, cap, 16)

    def peer_copy(k, source, target, sends, receives):
        return pltpu.make_async_remote_copy(
            source, target, sends.at[k], receives.at[k],
            device_id={"expert": flipped(me, k, groups)}, device_id_type=MESH,
        )

    def out_copy(k):
        return peer_copy(k, disp.at[flipped(me, k, groups)], recv.at[block_rows(k)], s_out, r_out)

    def back_copy(k):
        return peer_copy(k, raw_msg.at[k], back.at[me], s_back, r_back)

    def tail_copy(k):
        return peer_copy(k, tail_msg, tails.at[me], s_tail, r_tail)

    def cot_copy(k):
        return peer_copy(k, cot_msg.at[flipped(me, k, groups)], cot_in.at[k], s_cot, r_cot)

    def code_copy(k):
        return peer_copy(k, code_msg.at[flipped(me, k, groups)], code_in.at[k], s_code, r_code)

    def each(body):
        def turn(j, carry):
            body(turn_of(j))
            return carry

        lax.fori_loop(1, groups, turn, 0)

    spot = iota((4, LANES), 0) == iota((4, LANES), 1)
    lane = iota((4, LANES), 1)
    for h in range(2):
        tail = tail_rows(wt, h).astype(F32)
        column = jnp.sum(jnp.where(spot, tail[8:9, 0:LANES], 0.0), axis=1, keepdims=True)
        tail_msg[4 * h : 4 * h + 4, :] = jnp.where(
            lane < CODE_WIDTH, tail[4:8, 0:LANES], jnp.where(lane == CODE_WIDTH, column, 0.0)
        )
    tails[me] = tail_msg[...]
    pl.semaphore_wait(barrier, groups + 1)
    each(lambda k: tail_copy(k).start())
    each(lambda k: out_copy(k).start())

    m0[...] = jnp.zeros_like(m0)
    head[...] = jnp.zeros_like(head)
    for h in range(2):
        m0[h, ENC_WIDTH * h : ENC_WIDTH * (h + 1), :] = wt[h, 0:ENC_WIDTH, :]
        head[h, 4 * h : 4 * h + 4, :] = tail_rows(wt, h).astype(F32)[0:4]
    recv[block_rows(0), :] = disp[me]

    def process(k):
        block = block_rows(k)
        features = recv[block, :]
        biases = [tail_rows(wt, h).astype(F32) for h in range(2)]
        current = [features, features]
        for layer in range(LAYERS):
            for h in range(2):
                preact = dot(current[h], layer_matrix(wt, m0, h, layer))
                preact = preact + biases[h][9 + layer : 10 + layer, :]
                current[h] = jnp.maximum(preact, 0.0).astype(BF16)
                act[layer, h, block, :] = current[h]
        for h in range(2):
            raw = dot(tail_rows(wt, h), current[h], NT)
            raw_msg[k, 4 * h : 4 * h + 4, 0:cap] = raw[0:4]

    process(0)
    back[me] = raw_msg[0]

    for h in range(2):
        for layer in range(1, LAYERS):
            matrix = layer_matrix(wt, m0, h, layer)
            turned[layer - 1, h] = matrix.astype(F32).T.astype(BF16)

    cell = cell_ref[...]
    rank = rank_ref[...]
    row = iota((SAMPLES, LANES), 0)
    live = row < length_ref[...]
    place = jnp.where(live, rank, 0)
    tile = lax.div(place, LANES)
    lane_index = place - tile * LANES
    key = jnp.where(live, cell * tiles + tile, -1)
    table_rows = code_ref.shape[0]
    block_index = me * lax.axis_size("dp") + my_dp
    pick = (
        iota((table_rows, LANES), 0) == image_ref[...] - block_index * table_rows
    ).astype(F32)
    ray_code = exact(code_ref[...].astype(BF16).astype(F32), pick, TN)

    keys[...] = key.astype(F32)
    eight[0:SAMPLES, :] = lane_index.astype(F32)
    slot_lane = iota((LANES, LANES), 0).astype(F32)

    def spread(i, carry):
        line = jnp.broadcast_to(eight[pl.ds(i, 1), :], (LANES, LANES))
        spots[:, lane_block(i)] = jnp.where(line == slot_lane, 1.0, 0.0).astype(BF16)
        return carry

    lax.fori_loop(0, SAMPLES, spread, 0)

    def step(j, carry):
        k = turn_of(j)
        out_copy(k).wait_recv()
        process(k)
        back_copy(k).start()
        return carry

    lax.fori_loop(1, groups, step, 0)

    each(lambda k: tail_copy(k).wait_recv())

    def collect(g, carry):
        queries[rows_of(g, 8), :] = tails[g, :, 0:CODE_WIDTH]
        shift[rows_of(g, 8), :] = jnp.broadcast_to(
            tails[g, :, CODE_WIDTH : CODE_WIDTH + 1], (8, LANES)
        )
        return carry

    lax.fori_loop(0, groups, collect, 0)
    mix[...] = exact(queries[...], ray_code) + shift[...]
    zero = jnp.zeros((SAMPLES, LANES), F32)

    def add_code(g, codes):
        part = mix[rows_of(g, 8), :]
        codes = list(codes)
        for h in range(2):
            hit = cell == 2 * g + h
            for c in range(4):
                j = 4 * h + c
                codes[c] = jnp.where(hit, part[j : j + 1, :], codes[c])
        return tuple(codes)

    codes = lax.fori_loop(0, groups, add_code, (zero,) * 4)

    def take(g, raws):
        raws = list(raws)
        for t in range(tiles):
            piece = back[g, :, t * LANES : (t + 1) * LANES]
            for h in range(2):
                hit = key == (2 * g + h) * tiles + t
                for c in range(4):
                    j = 4 * h + c
                    line = jnp.broadcast_to(piece[j : j + 1, :], (SAMPLES, LANES))
                    found = jnp.take_along_axis(line, lane_index, axis=1)
                    raws[c] = jnp.where(hit, found, raws[c])
        return tuple(raws)

    raws = take(me, (zero,) * 4)

    def take_next(j, raws):
        k = turn_of(j)
        back_copy(k).wait_recv()
        return take(flipped(me, k, groups), raws)

    raws = lax.fori_loop(1, groups, take_next, raws)
    raws = [jnp.where(live, raws[c] + codes[c], 0.0) for c in range(4)]
    spacing = spacing_ref[...]
    density = jnp.maximum(raws[0], 0.0) + jnp.log1p(jnp.exp(-jnp.abs(raws[0])))
    colors = [jax.nn.sigmoid(raw) for raw in raws[1:]]
    tau = jnp.where(live, density * spacing, 0.0)
    before = prefix(tau, row, False) - tau
    through = jnp.exp(-before)
    fade = jnp.exp(-tau)
    weight = through * (1.0 - fade)
    gaps = [
        jnp.sum(weight * colors[c], axis=0, keepdims=True) - target_ref[c : c + 1, :]
        for c in range(3)
    ]
    loss_out[...] = 0.5 * (gaps[0] * gaps[0] + gaps[1] * gaps[1] + gaps[2] * gaps[2])
    pull = gaps[0] * colors[0] + gaps[1] * colors[1] + gaps[2] * colors[2]
    gain = pull * weight
    after = prefix(gain, row, True) - gain
    tau_grad = pull * through * fade - after
    grads = [tau_grad * spacing * jax.nn.sigmoid(raws[0])]
    for c in range(3):
        grads.append(gaps[c] * weight * colors[c] * (1.0 - colors[c]))
    for c in range(4):
        cot = jnp.where(live, grads[c], 0.0).astype(BF16).astype(F32)
        eight[pl.ds(c, SAMPLES, 8), :] = cot
        eight[pl.ds(4 + c, SAMPLES, 8), :] = cot
    mix[...] = jnp.zeros_like(mix)
    member = lax.div(iota((8, LANES), 0), 4) * tiles

    def widen(i, carry):
        value = eight[rows_of(i, 8), :]
        line = jnp.broadcast_to(keys[pl.ds(i, 1), :], (8, LANES))
        sums = [0.0] * groups
        for t in range(tiles):
            for pair in range(groups // 2):
                both = []
                for g in (2 * pair, 2 * pair + 1):
                    want = (member + (2 * g * tiles + t)).astype(F32)
                    chosen = jnp.where(line == want, value, 0.0)
                    sums[g] = sums[g] + chosen
                    both.append(chosen)
                start = (t * groups + 2 * pair) * 8
                wide[start : start + 16, lane_block(i)] = jnp.concatenate(both, axis=0).astype(BF16)
        for g in range(groups):
            mix[8 * g : 8 * g + 8, :] += sums[g]
        return carry

    lax.fori_loop(0, SAMPLES, widen, 0)
    slots = dot(wide[...], spots[...], NT)
    for t in range(tiles):
        for g in range(groups):
            start = (t * groups + g) * 8
            cot_msg[g, :, t * LANES : (t + 1) * LANES] = slots[start : start + 8].astype(BF16)
    each(lambda k: cot_copy(k).start())
    cot_in[0] = cot_msg[me]

    totals = mix[...]
    query_grad = exact(totals, ray_code, NT)
    for g in range(groups):
        code_msg[g, :, 0:CODE_WIDTH] = query_grad[8 * g : 8 * g + 8]
        code_msg[g, :, CODE_WIDTH:] = jnp.zeros((8, LANES - CODE_WIDTH), F32)
    each(lambda k: code_copy(k).start())
    code_in[0] = code_msg[me]
    table_grad = exact(exact(totals, pick, NT), queries[...], TN)
    new_code, new_first, new_second = adam_update(
        code_ref[...], table_grad, first_ref[...], second_ref[...]
    )
    code_out[...] = new_code
    first_out[...] = new_first
    second_out[...] = new_second

    starts = [0] + [ENC_WIDTH + layer * NET_WIDTH for layer in range(LAYERS)] + [HEAD_ROW + 16]
    chunks = [pl.ds(starts[j], starts[j + 1] - starts[j]) for j in range(LAYERS + 1)]

    def near_copy(j):
        return pltpu.make_async_remote_copy(
            grad.at[1 - core, chunks[j]], half_in.at[chunks[j]],
            s_sum.at[0, j], r_sum.at[0, j], device_id={"dp": near}, device_id_type=MESH,
        )

    def far_copy(j):
        return pltpu.make_async_remote_copy(
            sum_out.at[chunks[j]], sum_in.at[chunks[j]],
            s_sum.at[1, j], r_sum.at[1, j], device_id={"dp": far}, device_id_type=MESH,
        )

    def full_copy(j, which):
        return pltpu.make_async_remote_copy(
            full.at[which, chunks[j]], full.at[which, chunks[j]],
            s_sum.at[2, j], r_sum.at[2, j], device_id={"dp": near}, device_id_type=MESH,
        )

    def second_stage(j):
        near_copy(j).wait_recv()
        rows = chunks[j]
        sum_out[rows, :] = (grad[core, rows, :] + half_in[rows, :]).astype(BF16)
        far_copy(j).start()

    def third_stage(j):
        far_copy(j).wait_recv()
        rows = chunks[j]
        full[core, rows, :] = sum_out[rows, :].astype(F32) + sum_in[rows, :].astype(F32)
        full_copy(j, core).start()

    top = LAYERS - 1
    heads_bf = [head[h].astype(BF16) for h in range(2)]
    bias[...] = jnp.zeros_like(bias)
    cot_sum[...] = jnp.zeros_like(cot_sum)

    def mask_store(layer, h, block, up):
        value = jnp.where(act[layer, h, block, :].astype(F32) > 0, up, 0.0).astype(BF16)
        pre[layer, h, block, :] = value
        bias[layer, h] += jnp.sum(value.astype(F32).reshape(-1, 8, NET_WIDTH), axis=0)

    def first_back(k, carry):
        block = block_rows(k)
        cot = cot_in[k, :, 0:cap]
        sums = []
        for h in range(2):
            mask_store(top, h, block, dot(cot, heads_bf[h], TN))
            sums.append(carry[h] + dot(cot, act[top, h, block, :]))
        cot_sum[...] += jnp.broadcast_to(
            jnp.sum(cot.astype(F32), axis=1, keepdims=True), (8, LANES)
        )
        return tuple(sums)

    def next_back(j, carry):
        k = turn_of(j)
        cot_copy(k).wait_recv()
        return first_back(k, carry)

    zeros = jnp.zeros((8, NET_WIDTH), F32)
    hidden = lax.fori_loop(1, groups, next_back, first_back(0, (zeros, zeros)))

    pieces = 4
    size = recv.shape[0] // pieces
    for layer in reversed(range(LAYERS)):
        if layer < top:

            def onward(index, carry):
                block = rows_of(index, size, 16)
                for h in range(2):
                    mask_store(
                        layer, h, block, dot(pre[layer + 1, h, block, :], turned[layer, h])
                    )
                return carry

            lax.fori_loop(0, pieces, onward, 0)
        for h in range(2):
            if layer == 0:
                value = dot(recv[...], pre[0, h], TN)
                grad[h, 0:ENC_WIDTH, :] = value[ENC_WIDTH * h : ENC_WIDTH * (h + 1)]
            else:
                grad[h, chunks[layer], :] = dot(act[layer - 1, h], pre[layer, h], TN)
        near_copy(layer).start()
        if layer < top:
            second_stage(layer + 1)
        if layer < top - 1:
            third_stage(layer + 2)

    def add_codes(k, carry):
        code_copy(k).wait_recv()
        return carry + code_in[k]

    code_sum = lax.fori_loop(1, groups, add_codes, code_in[0])
    codes = jnp.concatenate([code_sum, jnp.zeros((8, NET_WIDTH - LANES), F32)], axis=1)
    spot = iota((8, LANES), 0) == iota((8, LANES), 1)
    cot_row = jnp.sum(jnp.where(spot, cot_sum[...], 0.0), axis=0, keepdims=True)
    lane = iota((1, LANES), 1)
    for h in range(2):
        line = cot_row if h == 0 else pltpu.roll(cot_row, LANES - 4, 1)
        line = jnp.where(lane < 4, line, 0.0)
        line = jnp.concatenate([line, jnp.zeros((1, NET_WIDTH - LANES), F32)], axis=1)
        grad[h, HEAD_ROW : HEAD_ROW + 16, :] = jnp.concatenate(
            [hidden[h][4 * h : 4 * h + 4], codes[4 * h : 4 * h + 4], line]
            + [jnp.sum(bias[layer, h], axis=0, keepdims=True) for layer in range(LAYERS)]
            + [jnp.zeros((7 - LAYERS, NET_WIDTH), F32)],
            axis=0,
        )
    near_copy(LAYERS).start()
    second_stage(0)
    third_stage(1)
    second_stage(LAYERS)
    third_stage(0)
    third_stage(LAYERS)

    def drain(k):
        for copy in (tail_copy, out_copy, back_copy, cot_copy, code_copy):
            copy(k).wait_send()

    each(drain)
    for j in (3, 2, 1, 0, LAYERS):
        near_copy(j).wait_send()
        far_copy(j).wait_send()
        full_copy(j, core).wait_send()
        full_copy(j, 1 - core).wait_recv()
        grad_out[:, chunks[j], :] = full[:, chunks[j], :]


def update_kernel(*refs):
    grad, params, first, second = refs[:4]
    smalls, large_outs, small_outs = refs[4:8], refs[8:11], refs[11:15]
    stages, large_sems, small_sems = refs[15:18], refs[18], refs[19]
    copies = [
        pltpu.make_async_copy(source, target, small_sems.at[n])
        for n, (source, target) in enumerate(zip(smalls, small_outs))
    ]
    for copy in copies:
        copy.start()
    half = grad.shape[1] // 2
    for part in range(4):
        rows = pl.ds(part % 2 * half, half)
        spot = (part // 2, rows, slice(None))
        values = adam_update(params[spot], grad[spot], first[spot], second[spot])
        for n in range(3):
            stages[n][spot] = values[n]
            copy = pltpu.make_async_copy(
                stages[n].at[spot], large_outs[n].at[spot], large_sems.at[n, part]
            )
            copy.start()
            copies.append(copy)
    for copy in copies:
        copy.wait()


def shards(
    features, spacing, targets, ray_length, cell_id, slot_rank, image_id,
    params, first_moment, second_moment, code_table, table_first, table_second,
):
    ray_rows = features.shape[0]
    sample_count = ray_rows * SAMPLES
    groups = lax.axis_size("expert")
    experts_all = params.shape[0] * groups
    cap = 2 * (sample_count * 3 // 4 // experts_all)
    cap_up = -(-cap // LANES) * LANES
    tiles = cap_up // LANES
    wide_rows = tiles * groups * 8
    slots_up = experts_all * cap_up
    shape = jax.ShapeDtypeStruct
    scratch = pltpu.VMEM
    sem = pltpu.SemaphoreType.DMA
    smalls = [
        spacing.T, ray_length[None, :], targets, image_id[None, :],
        code_table, table_first, table_second,
    ]
    inputs = [cell_id.T, slot_rank.T, features.transpose(1, 2, 0), params] + smalls
    inputs = [pltpu.with_memory_space_constraint(value, pltpu.HBM) for value in inputs]
    like = lambda value: shape(value.shape, value.dtype)
    *placed, master = pl.pallas_call(
        functools.partial(place_kernel, groups, cap, cap_up),
        out_shape=[
            shape((groups, cap, LANES), BF16), shape(params.shape, BF16),
            like(inputs[0]), like(inputs[1]),
        ] + [like(value) for value in smalls + [params]],
        in_specs=[HBM] * len(inputs),
        out_specs=[VMEM] * (5 + len(smalls)),
        scratch_shapes=[
            scratch((SAMPLES, ENC_WIDTH, ray_rows), BF16),
            scratch((sample_count, LANES), F32),
            scratch((slots_up + 8, LANES), F32),
            scratch((experts_all, LANES), F32),
            scratch((SAMPLES, LANES), jnp.int32),
            pltpu.SMEM((SAMPLES, LANES), jnp.int32),
            sem((len(inputs),)), sem,
        ],
        compiler_params=pltpu.CompilerParams(vmem_limit_bytes=12 * 2**20),
        cost_estimate=pl.CostEstimate(flops=0, bytes_accessed=6000 * sample_count, transcendentals=0),
        name="place",
    )(*inputs)
    all_rows = groups * cap
    grad_rows = params.shape[1]
    table_shape = shape(code_table.shape, F32)
    peers = sem((groups,))
    param_grad, loss, new_table, new_table_first, new_table_second = pl.pallas_call(
        functools.partial(step_kernel, groups, cap, cap_up),
        out_shape=(
            shape(params.shape, F32), shape((1, ray_rows), F32), table_shape, table_shape, table_shape,
        ),
        in_specs=[VMEM] * 11,
        out_specs=(VMEM,) * 5,
        scratch_shapes=[
            scratch((2, LANES, NET_WIDTH), BF16),
            scratch((LAYERS - 1, 2, NET_WIDTH, NET_WIDTH), BF16),
            scratch((2, 8, NET_WIDTH), F32),
            scratch((all_rows, LANES), BF16),
            scratch((LAYERS, 2, all_rows, NET_WIDTH), BF16),
            scratch((LAYERS, 2, all_rows, NET_WIDTH), BF16),
            scratch((groups, 8, cap_up), F32),
            scratch((groups, 8, cap_up), F32),
            scratch((8, LANES), F32),
            scratch((groups, 8, LANES), F32),
            scratch((8 * groups, CODE_WIDTH), F32),
            scratch((8 * groups, LANES), F32),
            scratch((8 * groups, LANES), F32),
            scratch((8 * SAMPLES, LANES), F32),
            scratch((SAMPLES, LANES), F32),
            scratch((wide_rows, sample_count), BF16),
            scratch((LANES, sample_count), BF16),
            scratch((groups, 8, cap_up), BF16),
            scratch((groups, 8, cap_up), BF16),
            scratch((groups, 8, LANES), F32),
            scratch((groups, 8, LANES), F32),
            scratch((8, LANES), F32),
            scratch((LAYERS, 2, 8, NET_WIDTH), F32),
            scratch((2, grad_rows, NET_WIDTH), F32),
            scratch((grad_rows, NET_WIDTH), F32),
            scratch((grad_rows, NET_WIDTH), BF16),
            scratch((grad_rows, NET_WIDTH), BF16),
            scratch((2, grad_rows, NET_WIDTH), F32),
            peers, peers, peers, peers, peers, peers, peers, peers, peers, peers,
            sem((3, LAYERS + 1)),
            sem((3, LAYERS + 1)),
        ],
        compiler_params=pltpu.CompilerParams(
            collective_id=0, has_side_effects=True, vmem_limit_bytes=36 * 2**20 + 2 * wide_rows * sample_count
        ),
        cost_estimate=pl.CostEstimate(flops=0, bytes_accessed=50000 * sample_count, transcendentals=0),
        name="step",
    )(*placed)
    whole = shape(params.shape, F32)
    new_params, new_first, new_second, loss, *tables = pl.pallas_call(
        update_kernel,
        out_shape=[whole] * 3 + [shape((1, ray_rows), F32)] + [table_shape] * 3,
        in_specs=[VMEM] * 8,
        out_specs=[HBM] * 7,
        scratch_shapes=[scratch(params.shape, F32)] * 3 + [sem((3, 4)), sem((4,))],
        compiler_params=pltpu.CompilerParams(vmem_limit_bytes=16 * 2**20),
        name="update",
    )(
        param_grad, master, first_moment, second_moment, loss,
        new_table, new_table_first, new_table_second,
    )
    return (loss.reshape(ray_rows), new_params, new_first, new_second, *tables)


def solution(mesh):
    both = ("expert", "dp")
    return jax.shard_map(
        shards,
        mesh=mesh,
        in_specs=(
            P(both, None, None), P(both, None), P(None, both), P(both), P(both, None),
            P(both, None), P(both),
            P("expert", None, None), P("expert", None, None), P("expert", None, None),
            P(both, None), P(both, None), P(both, None),
        ),
        out_specs=(
            P(both),
            P("expert", None, None), P("expert", None, None), P("expert", None, None),
            P(both, None), P(both, None), P(both, None),
        ),
        check_vma=False,
    )
```

```python
import functools
import math

import jax
import jax.numpy as jnp
from jax import lax
from jax.experimental import pallas as pl
from jax.experimental.pallas import tpu as pltpu
from jax.sharding import PartitionSpec as P

NET_WIDTH = 256
CODE_WIDTH = 64
ENC_WIDTH = 64
LAYERS = 4
SAMPLES = 32
HEAD_ROW = ENC_WIDTH + (LAYERS - 1) * NET_WIDTH
LANES = 128

BETA_ONE = 0.9
BETA_TWO = 0.999
LEARN_RATE = 0.001
ADAM_EPS = 1e-08
CORRECT_ONE = 1.0 - 0.9**10
CORRECT_TWO = 1.0 - 0.999**10

MESH = pl.DeviceIdType.MESH
VMEM = pl.BlockSpec(memory_space=pltpu.VMEM)
HBM = pl.BlockSpec(memory_space=pltpu.HBM)
F32 = jnp.float32
BF16 = jnp.bfloat16
NN = (((1,), (0,)), ((), ()))
NT = (((1,), (1,)), ((), ()))
TN = (((0,), (0,)), ((), ()))


def dot(left, right, dims=NN, precision=None):
    return lax.dot_general(left, right, dims, precision=precision, preferred_element_type=F32)


def exact(left, right, dims=NN):
    return dot(left, right, dims, lax.Precision.HIGHEST)


def adam_update(param_now, gradient, moment_one, moment_two):
    new_one = BETA_ONE * moment_one + (1.0 - BETA_ONE) * gradient
    new_two = BETA_TWO * moment_two + (1.0 - BETA_TWO) * gradient * gradient
    update = LEARN_RATE * (new_one / CORRECT_ONE) / (jnp.sqrt(new_two / CORRECT_TWO) + ADAM_EPS)
    return (param_now - update, new_one, new_two)


def iota(shape, dim):
    return lax.broadcasted_iota(jnp.int32, shape, dim)


def lane_block(index):
    return pl.ds(pl.multiple_of(index * LANES, LANES), LANES)


def rows_of(index, count, align=8):
    return pl.ds(pl.multiple_of(index * count, align), count)


def place_kernel(
    groups, cap, cap_up, cell_hbm, rank_hbm, feat_hbm, params_hbm, *refs,
):
    smalls = refs[:7]
    out_ref, wt, cell_ref, rank_ref = refs[7:11]
    small_outs = refs[11:18]
    master, feat, rows, table, counts, slot_vec, slot, load_sems, slot_sem = refs[18:]
    pairs = [(cell_hbm, cell_ref), (rank_hbm, rank_ref), (feat_hbm, feat), (params_hbm, master)]
    pairs += list(zip(smalls, small_outs))
    loads = [
        pltpu.make_async_copy(source, target, load_sems.at[n])
        for n, (source, target) in enumerate(pairs)
    ]
    for load in loads:
        load.start()
    loads[0].wait()
    loads[1].wait()
    cell = cell_ref[...]
    rank = rank_ref[...]
    live = rank >= 0
    slot_vec[...] = jnp.where(live, cell * cap_up + rank, 2 * groups * cap_up)
    scalars = pltpu.make_async_copy(slot_vec, slot, slot_sem)
    scalars.start()
    kind = jnp.where(live, cell, -1)

    def count(g, carry):
        parts = [
            jnp.sum(jnp.where(kind == 8 * g + j, 1.0, 0.0), axis=0, keepdims=True)
            for j in range(8)
        ]
        total = jnp.sum(jnp.concatenate(parts, axis=0), axis=1, keepdims=True)
        counts[rows_of(g, 8), :] = jnp.broadcast_to(total, (8, LANES))
        return carry

    lax.fori_loop(0, 2 * groups // 8, count, 0)
    loads[2].wait()

    def turn(index, carry):
        for inner in range(4):
            i = index * 4 + inner
            block = feat[i].astype(F32)
            rows[lane_block(i), :] = jnp.concatenate([block, block], axis=0).T
        return carry

    lax.fori_loop(0, SAMPLES // 4, turn, 0)
    scalars.wait()
    for i in range(SAMPLES):

        def move(r, carry):
            table[pl.ds(slot[i, r], 1), :] = rows[pl.ds(i * LANES + r, 1), :]
            return carry

        lax.fori_loop(0, LANES, move, 0, unroll=True)
    low = iota((1, LANES), 1) < ENC_WIDTH
    position = iota((cap, LANES), 0).astype(F32)

    def pack(g, carry):
        first = table[pl.ds(pl.multiple_of(2 * g * cap_up, LANES), cap), :]
        second = table[pl.ds(pl.multiple_of((2 * g + 1) * cap_up, LANES), cap), :]
        limit = jnp.where(low, counts[pl.ds(2 * g, 1), :], counts[pl.ds(2 * g + 1, 1), :])
        value = jnp.where(low, first, second)
        out_ref[g] = jnp.where(position < limit, value, 0.0).astype(BF16)
        return carry

    lax.fori_loop(0, groups, pack, 0)
    for load in loads[3:]:
        load.wait()
    wt[...] = master[...].astype(BF16)


def flipped(me, k, groups):
    peer = 0
    bit = 1
    while bit < groups:
        peer = peer + bit * lax.rem(lax.div(me, bit) + lax.div(k, bit), 2)
        bit *= 2
    return peer


def layer_matrix(wt, m0, h, layer):
    if layer == 0:
        return m0[h]
    start = ENC_WIDTH + (layer - 1) * NET_WIDTH
    return wt[h, start : start + NET_WIDTH, :]


def tail_rows(wt, h):
    return wt[h, HEAD_ROW : HEAD_ROW + 16, :]


def prefix(value, row, backwards):
    step = 1
    while step < SAMPLES:
        if backwards:
            moved = jnp.where(row < SAMPLES - step, pltpu.roll(value, SAMPLES - step, 0), 0.0)
        else:
            moved = jnp.where(row >= step, pltpu.roll(value, step, 0), 0.0)
        value = value + moved
        step *= 2
    return value


def step_kernel(
    groups, cap, cap_up,
    disp, wt, cell_ref, rank_ref, spacing_ref, length_ref, target_ref, image_ref,
    code_ref, first_ref, second_ref,
    grad_out, loss_out, code_out, first_out, second_out,
    m0, turned, head, recv, act, act_t, feat_t, pre,
    raw_msg, back, tail_msg, tails, queries, shift, mix, eight, keys, wide, spots,
    cot_msg, cot_in, code_msg, code_in, cot_sum, bias, grad, half_in, sum_out, sum_in, full,
    s_out, r_out, s_back, r_back, s_tail, r_tail, s_cot, r_cot, s_code, r_code,
    s_sum, r_sum,
):
    tiles = cap_up // LANES
    batch = LANES // math.gcd(cap, LANES)
    me = lax.axis_index("expert")
    my_dp = lax.axis_index("dp")
    core = lax.rem(my_dp, 2)
    near = my_dp + 1 - 2 * core
    far = my_dp + 2 - 4 * lax.rem(lax.div(my_dp, 2), 2)
    barrier = pltpu.get_barrier_semaphore()

    def greet(k, carry):
        pl.semaphore_signal(
            barrier, 1, device_id={"expert": lax.rem(me + k, groups)}, device_id_type=MESH
        )
        return carry

    lax.fori_loop(1, groups, greet, 0)
    for peer in (near, far):
        pl.semaphore_signal(barrier, 1, device_id={"dp": peer}, device_id_type=MESH)

    def turn_of(j):
        return j

    def block_rows(k):
        return rows_of(k, cap, 16)

    def peer_copy(k, source, target, sends, receives):
        return pltpu.make_async_remote_copy(
            source, target, sends.at[k], receives.at[k],
            device_id={"expert": flipped(me, k, groups)}, device_id_type=MESH,
        )

    def out_copy(k):
        return peer_copy(k, disp.at[flipped(me, k, groups)], recv.at[block_rows(k)], s_out, r_out)

    def back_copy(k):
        return peer_copy(k, raw_msg.at[k], back.at[me], s_back, r_back)

    def tail_copy(k):
        return peer_copy(k, tail_msg, tails.at[me], s_tail, r_tail)

    def cot_copy(k):
        return peer_copy(k, cot_msg.at[flipped(me, k, groups)], cot_in.at[k], s_cot, r_cot)

    def code_copy(k):
        return peer_copy(k, code_msg.at[flipped(me, k, groups)], code_in.at[k], s_code, r_code)

    def each(body):
        def turn(j, carry):
            body(turn_of(j))
            return carry

        lax.fori_loop(1, groups, turn, 0)

    spot = iota((4, LANES), 0) == iota((4, LANES), 1)
    lane = iota((4, LANES), 1)
    for h in range(2):
        tail = tail_rows(wt, h).astype(F32)
        column = jnp.sum(jnp.where(spot, tail[8:9, 0:LANES], 0.0), axis=1, keepdims=True)
        tail_msg[4 * h : 4 * h + 4, :] = jnp.where(
            lane < CODE_WIDTH, tail[4:8, 0:LANES], jnp.where(lane == CODE_WIDTH, column, 0.0)
        )
    tails[me] = tail_msg[...]
    pl.semaphore_wait(barrier, groups + 1)
    each(lambda k: tail_copy(k).start())
    each(lambda k: out_copy(k).start())

    m0[...] = jnp.zeros_like(m0)
    head[...] = jnp.zeros_like(head)
    ones = jnp.ones((16, recv.shape[0]), BF16)
    feat_t[LANES:, :] = ones
    for layer in range(LAYERS - 1):
        for h in range(2):
            act_t[layer, h, NET_WIDTH:, :] = ones
    for h in range(2):
        m0[h, ENC_WIDTH * h : ENC_WIDTH * (h + 1), :] = wt[h, 0:ENC_WIDTH, :]
        head[h, 4 * h : 4 * h + 4, :] = tail_rows(wt, h).astype(F32)[0:4]
    recv[block_rows(0), :] = disp[me]

    def process(k):
        block = block_rows(k)
        features = recv[block, :]
        biases = [tail_rows(wt, h).astype(F32) for h in range(2)]
        current = [features, features]
        for layer in range(LAYERS):
            for h in range(2):
                preact = dot(current[h], layer_matrix(wt, m0, h, layer))
                preact = preact + biases[h][9 + layer : 10 + layer, :]
                current[h] = jnp.maximum(preact, 0.0).astype(BF16)
                act[layer, h, block, :] = current[h]
        for h in range(2):
            raw = dot(tail_rows(wt, h), current[h], NT)
            raw_msg[k, 4 * h : 4 * h + 4, 0:cap] = raw[0:4]

    process(0)
    back[me] = raw_msg[0]

    for h in range(2):
        for layer in range(1, LAYERS):
            matrix = layer_matrix(wt, m0, h, layer)
            turned[layer - 1, h] = matrix.astype(F32).T.astype(BF16)

    cell = cell_ref[...]
    rank = rank_ref[...]
    row = iota((SAMPLES, LANES), 0)
    live = row < length_ref[...]
    place = jnp.where(live, rank, 0)
    tile = lax.div(place, LANES)
    lane_index = place - tile * LANES
    key = jnp.where(live, cell * tiles + tile, -1)
    table_rows = code_ref.shape[0]
    block_index = me * lax.axis_size("dp") + my_dp
    pick = (
        iota((table_rows, LANES), 0) == image_ref[...] - block_index * table_rows
    ).astype(F32)
    ray_code = exact(code_ref[...].astype(BF16).astype(F32), pick, TN)

    keys[...] = key.astype(F32)
    eight[0:SAMPLES, :] = lane_index.astype(F32)
    slot_lane = iota((LANES, LANES), 0).astype(F32)

    def spread(i, carry):
        line = jnp.broadcast_to(eight[pl.ds(i, 1), :], (LANES, LANES))
        spots[:, lane_block(i)] = jnp.where(line == slot_lane, 1.0, 0.0).astype(BF16)
        return carry

    lax.fori_loop(0, SAMPLES, spread, 0)

    def transpose(c):
        rows = rows_of(c, batch * cap, 16)
        lanes = pl.ds(pl.multiple_of(c * batch * cap, LANES), batch * cap)
        feat_t[0:LANES, lanes] = recv[rows, :].T
        for layer in range(LAYERS - 1):
            for h in range(2):
                act_t[layer, h, 0:NET_WIDTH, lanes] = act[layer, h, rows, :].T

    def receive(k, carry):
        out_copy(k).wait_recv()
        process(k)
        back_copy(k).start()
        return carry

    def receive_batch(c, carry):
        if batch == 1:
            receive(c, carry)
        else:
            lax.fori_loop(c * batch, (c + 1) * batch, receive, 0)
        transpose(c)
        return carry

    lax.fori_loop(1, batch, receive, 0)
    transpose(0)
    lax.fori_loop(1, groups // batch, receive_batch, 0)

    each(lambda k: tail_copy(k).wait_recv())

    def collect(g, carry):
        queries[rows_of(g, 8), :] = tails[g, :, 0:CODE_WIDTH]
        shift[rows_of(g, 8), :] = jnp.broadcast_to(
            tails[g, :, CODE_WIDTH : CODE_WIDTH + 1], (8, LANES)
        )
        return carry

    lax.fori_loop(0, groups, collect, 0)
    mix[...] = exact(queries[...], ray_code) + shift[...]
    zero = jnp.zeros((SAMPLES, LANES), F32)

    def add_code(g, codes):
        part = mix[rows_of(g, 8), :]
        codes = list(codes)
        for h in range(2):
            hit = cell == 2 * g + h
            for c in range(4):
                j = 4 * h + c
                codes[c] = jnp.where(hit, part[j : j + 1, :], codes[c])
        return tuple(codes)

    codes = lax.fori_loop(0, groups, add_code, (zero,) * 4)

    def take(g, raws):
        raws = list(raws)
        for t in range(tiles):
            piece = back[g, :, t * LANES : (t + 1) * LANES]
            for h in range(2):
                hit = key == (2 * g + h) * tiles + t
                for c in range(4):
                    j = 4 * h + c
                    line = jnp.broadcast_to(piece[j : j + 1, :], (SAMPLES, LANES))
                    found = jnp.take_along_axis(line, lane_index, axis=1)
                    raws[c] = jnp.where(hit, found, raws[c])
        return tuple(raws)

    raws = take(me, (zero,) * 4)

    def take_next(j, raws):
        k = turn_of(j)
        back_copy(k).wait_recv()
        return take(flipped(me, k, groups), raws)

    raws = lax.fori_loop(1, groups, take_next, raws)
    raws = [jnp.where(live, raws[c] + codes[c], 0.0) for c in range(4)]
    spacing = spacing_ref[...]
    density = jnp.maximum(raws[0], 0.0) + jnp.log1p(jnp.exp(-jnp.abs(raws[0])))
    colors = [jax.nn.sigmoid(raw) for raw in raws[1:]]
    tau = jnp.where(live, density * spacing, 0.0)
    before = prefix(tau, row, False) - tau
    through = jnp.exp(-before)
    fade = jnp.exp(-tau)
    weight = through * (1.0 - fade)
    gaps = [
        jnp.sum(weight * colors[c], axis=0, keepdims=True) - target_ref[c : c + 1, :]
        for c in range(3)
    ]
    loss_out[...] = 0.5 * (gaps[0] * gaps[0] + gaps[1] * gaps[1] + gaps[2] * gaps[2])
    pull = gaps[0] * colors[0] + gaps[1] * colors[1] + gaps[2] * colors[2]
    gain = pull * weight
    after = prefix(gain, row, True) - gain
    tau_grad = pull * through * fade - after
    grads = [tau_grad * spacing * jax.nn.sigmoid(raws[0])]
    for c in range(3):
        grads.append(gaps[c] * weight * colors[c] * (1.0 - colors[c]))
    for c in range(4):
        cot = jnp.where(live, grads[c], 0.0).astype(BF16).astype(F32)
        eight[pl.ds(c, SAMPLES, 8), :] = cot
        eight[pl.ds(4 + c, SAMPLES, 8), :] = cot
    mix[...] = jnp.zeros_like(mix)
    member = lax.div(iota((8, LANES), 0), 4) * tiles

    def widen(i, carry):
        value = eight[rows_of(i, 8), :]
        line = jnp.broadcast_to(keys[pl.ds(i, 1), :], (8, LANES))
        sums = [0.0] * groups
        for t in range(tiles):
            for pair in range(groups // 2):
                both = []
                for g in (2 * pair, 2 * pair + 1):
                    want = (member + (2 * g * tiles + t)).astype(F32)
                    chosen = jnp.where(line == want, value, 0.0)
                    sums[g] = sums[g] + chosen
                    both.append(chosen)
                start = (t * groups + 2 * pair) * 8
                wide[start : start + 16, lane_block(i)] = jnp.concatenate(both, axis=0).astype(BF16)
        for g in range(groups):
            mix[8 * g : 8 * g + 8, :] += sums[g]
        return carry

    lax.fori_loop(0, SAMPLES, widen, 0)
    slots = dot(wide[...], spots[...], NT)
    for t in range(tiles):
        for g in range(groups):
            start = (t * groups + g) * 8
            cot_msg[g, :, t * LANES : (t + 1) * LANES] = slots[start : start + 8].astype(BF16)
    each(lambda k: cot_copy(k).start())
    cot_in[0] = cot_msg[me]

    totals = mix[...]
    query_grad = exact(totals, ray_code, NT)
    for g in range(groups):
        code_msg[g, :, 0:CODE_WIDTH] = query_grad[8 * g : 8 * g + 8]
        code_msg[g, :, CODE_WIDTH:] = jnp.zeros((8, LANES - CODE_WIDTH), F32)
    each(lambda k: code_copy(k).start())
    code_in[0] = code_msg[me]
    table_grad = exact(exact(totals, pick, NT), queries[...], TN)
    new_code, new_first, new_second = adam_update(
        code_ref[...], table_grad, first_ref[...], second_ref[...]
    )
    code_out[...] = new_code
    first_out[...] = new_first
    second_out[...] = new_second

    starts = [0] + [ENC_WIDTH + layer * NET_WIDTH for layer in range(LAYERS)] + [HEAD_ROW + 16]
    chunks = [pl.ds(starts[j], starts[j + 1] - starts[j]) for j in range(LAYERS + 1)]

    def near_copy(j):
        return pltpu.make_async_remote_copy(
            grad.at[1 - core, chunks[j]], half_in.at[chunks[j]],
            s_sum.at[0, j], r_sum.at[0, j], device_id={"dp": near}, device_id_type=MESH,
        )

    def far_copy(j):
        return pltpu.make_async_remote_copy(
            sum_out.at[chunks[j]], sum_in.at[chunks[j]],
            s_sum.at[1, j], r_sum.at[1, j], device_id={"dp": far}, device_id_type=MESH,
        )

    def full_copy(j, which):
        return pltpu.make_async_remote_copy(
            full.at[which, chunks[j]], full.at[which, chunks[j]],
            s_sum.at[2, j], r_sum.at[2, j], device_id={"dp": near}, device_id_type=MESH,
        )

    def second_stage(j):
        near_copy(j).wait_recv()
        rows = chunks[j]
        sum_out[rows, :] = (grad[core, rows, :] + half_in[rows, :]).astype(BF16)
        far_copy(j).start()

    def third_stage(j):
        far_copy(j).wait_recv()
        rows = chunks[j]
        full[core, rows, :] = sum_out[rows, :].astype(F32) + sum_in[rows, :].astype(F32)
        full_copy(j, core).start()

    top = LAYERS - 1
    heads_bf = [head[h].astype(BF16) for h in range(2)]
    cot_sum[...] = jnp.zeros_like(cot_sum)

    def mask_store(layer, h, block, up):
        up = up.astype(BF16)
        pre[layer, h, block, :] = jnp.where(act[layer, h, block, :] > 0, up, jnp.zeros_like(up))

    def first_back(k, carry):
        block = block_rows(k)
        cot = cot_in[k, :, 0:cap]
        sums = []
        for h in range(2):
            mask_store(top, h, block, dot(cot, heads_bf[h], TN))
            sums.append(carry[h] + dot(cot, act[top, h, block, :]))
        cot_sum[...] += jnp.broadcast_to(
            jnp.sum(cot.astype(F32), axis=1, keepdims=True), (8, LANES)
        )
        return tuple(sums)

    def next_back(j, carry):
        k = turn_of(j)
        cot_copy(k).wait_recv()
        return first_back(k, carry)

    zeros = jnp.zeros((8, NET_WIDTH), F32)
    hidden = lax.fori_loop(1, groups, next_back, first_back(0, (zeros, zeros)))

    pieces = 4
    size = recv.shape[0] // pieces
    for layer in reversed(range(LAYERS)):
        if layer < top:

            def onward(index, carry):
                block = rows_of(index, size, 16)
                for h in range(2):
                    mask_store(
                        layer, h, block, dot(pre[layer + 1, h, block, :], turned[layer, h])
                    )
                return carry

            lax.fori_loop(0, pieces // 2, onward, 0)
            second_stage(layer + 1)
            lax.fori_loop(pieces // 2, pieces, onward, 0)
        if layer == 0:
            for h in range(2):
                value = dot(feat_t[...], pre[0, h])
                bias[0, h, 0:1, :] = value[LANES : LANES + 1]
                grad[h, 0:ENC_WIDTH, :] = value[ENC_WIDTH * h : ENC_WIDTH * (h + 1)]
            near_copy(0).start()
        else:
            for h in (1 - core, core):
                value = dot(act_t[layer - 1, h], pre[layer, h])
                bias[layer, h, 0:1, :] = value[NET_WIDTH : NET_WIDTH + 1]
                grad[h, chunks[layer], :] = value[0:NET_WIDTH]
                if h is not core:
                    near_copy(layer).start()
        if layer < top - 1:
            third_stage(layer + 2)

    def add_codes(k, carry):
        code_copy(k).wait_recv()
        return carry + code_in[k]

    code_sum = lax.fori_loop(1, groups, add_codes, code_in[0])
    codes = jnp.concatenate([code_sum, jnp.zeros((8, NET_WIDTH - LANES), F32)], axis=1)
    spot = iota((8, LANES), 0) == iota((8, LANES), 1)
    cot_row = jnp.sum(jnp.where(spot, cot_sum[...], 0.0), axis=0, keepdims=True)
    lane = iota((1, LANES), 1)
    for h in range(2):
        line = cot_row if h == 0 else pltpu.roll(cot_row, LANES - 4, 1)
        line = jnp.where(lane < 4, line, 0.0)
        line = jnp.concatenate([line, jnp.zeros((1, NET_WIDTH - LANES), F32)], axis=1)
        grad[h, HEAD_ROW : HEAD_ROW + 16, :] = jnp.concatenate(
            [hidden[h][4 * h : 4 * h + 4], codes[4 * h : 4 * h + 4], line]
            + [bias[layer, h, 0:1, :] for layer in range(LAYERS)]
            + [jnp.zeros((7 - LAYERS, NET_WIDTH), F32)],
            axis=0,
        )
    near_copy(LAYERS).start()
    second_stage(0)
    second_stage(LAYERS)
    third_stage(1)
    third_stage(0)
    third_stage(LAYERS)

    def drain(k):
        for copy in (tail_copy, out_copy, back_copy, cot_copy, code_copy):
            copy(k).wait_send()

    each(drain)
    for j in (3, 2, 1, 0, LAYERS):
        near_copy(j).wait_send()
        far_copy(j).wait_send()
        full_copy(j, core).wait_send()
        full_copy(j, 1 - core).wait_recv()
        grad_out[:, chunks[j], :] = full[:, chunks[j], :]


def update_kernel(*refs):
    grad, params, first, second = refs[:4]
    smalls, large_outs, small_outs = refs[4:8], refs[8:11], refs[11:15]
    stages, large_sems, small_sems = refs[15:18], refs[18], refs[19]
    copies = [
        pltpu.make_async_copy(source, target, small_sems.at[n])
        for n, (source, target) in enumerate(zip(smalls, small_outs))
    ]
    for copy in copies:
        copy.start()
    half = grad.shape[1] // 2
    for part in range(4):
        rows = pl.ds(part % 2 * half, half)
        spot = (part // 2, rows, slice(None))
        values = adam_update(params[spot], grad[spot], first[spot], second[spot])
        for n in range(3):
            stages[n][spot] = values[n]
            copy = pltpu.make_async_copy(
                stages[n].at[spot], large_outs[n].at[spot], large_sems.at[n, part]
            )
            copy.start()
            copies.append(copy)
    for copy in copies:
        copy.wait()


def shards(
    features, spacing, targets, ray_length, cell_id, slot_rank, image_id,
    params, first_moment, second_moment, code_table, table_first, table_second,
):
    ray_rows = features.shape[0]
    sample_count = ray_rows * SAMPLES
    groups = lax.axis_size("expert")
    experts_all = params.shape[0] * groups
    cap = 2 * (sample_count * 3 // 4 // experts_all)
    cap_up = -(-cap // LANES) * LANES
    tiles = cap_up // LANES
    wide_rows = tiles * groups * 8
    slots_up = experts_all * cap_up
    shape = jax.ShapeDtypeStruct
    scratch = pltpu.VMEM
    sem = pltpu.SemaphoreType.DMA
    smalls = [
        spacing.T, ray_length[None, :], targets, image_id[None, :],
        code_table, table_first, table_second,
    ]
    inputs = [cell_id.T, slot_rank.T, features.transpose(1, 2, 0), params] + smalls
    inputs = [pltpu.with_memory_space_constraint(value, pltpu.HBM) for value in inputs]
    like = lambda value: shape(value.shape, value.dtype)
    *placed, master = pl.pallas_call(
        functools.partial(place_kernel, groups, cap, cap_up),
        out_shape=[
            shape((groups, cap, LANES), BF16), shape(params.shape, BF16),
            like(inputs[0]), like(inputs[1]),
        ] + [like(value) for value in smalls + [params]],
        in_specs=[HBM] * len(inputs),
        out_specs=[VMEM] * (5 + len(smalls)),
        scratch_shapes=[
            scratch((SAMPLES, ENC_WIDTH, ray_rows), BF16),
            scratch((sample_count, LANES), F32),
            scratch((slots_up + 8, LANES), F32),
            scratch((experts_all, LANES), F32),
            scratch((SAMPLES, LANES), jnp.int32),
            pltpu.SMEM((SAMPLES, LANES), jnp.int32),
            sem((len(inputs),)), sem,
        ],
        compiler_params=pltpu.CompilerParams(vmem_limit_bytes=12 * 2**20),
        cost_estimate=pl.CostEstimate(flops=0, bytes_accessed=6000 * sample_count, transcendentals=0),
        name="place",
    )(*inputs)
    all_rows = groups * cap
    grad_rows = params.shape[1]
    table_shape = shape(code_table.shape, F32)
    peers = sem((groups,))
    param_grad, loss, new_table, new_table_first, new_table_second = pl.pallas_call(
        functools.partial(step_kernel, groups, cap, cap_up),
        out_shape=(
            shape(params.shape, F32), shape((1, ray_rows), F32), table_shape, table_shape, table_shape,
        ),
        in_specs=[VMEM] * 11,
        out_specs=(VMEM,) * 5,
        scratch_shapes=[
            scratch((2, LANES, NET_WIDTH), BF16),
            scratch((LAYERS - 1, 2, NET_WIDTH, NET_WIDTH), BF16),
            scratch((2, 8, NET_WIDTH), F32),
            scratch((all_rows, LANES), BF16),
            scratch((LAYERS, 2, all_rows, NET_WIDTH), BF16),
            scratch((LAYERS - 1, 2, NET_WIDTH + 16, all_rows), BF16),
            scratch((LANES + 16, all_rows), BF16),
            scratch((LAYERS, 2, all_rows, NET_WIDTH), BF16),
            scratch((groups, 8, cap_up), F32),
            scratch((groups, 8, cap_up), F32),
            scratch((8, LANES), F32),
            scratch((groups, 8, LANES), F32),
            scratch((8 * groups, CODE_WIDTH), F32),
            scratch((8 * groups, LANES), F32),
            scratch((8 * groups, LANES), F32),
            scratch((8 * SAMPLES, LANES), F32),
            scratch((SAMPLES, LANES), F32),
            scratch((wide_rows, sample_count), BF16),
            scratch((LANES, sample_count), BF16),
            scratch((groups, 8, cap_up), BF16),
            scratch((groups, 8, cap_up), BF16),
            scratch((groups, 8, LANES), F32),
            scratch((groups, 8, LANES), F32),
            scratch((8, LANES), F32),
            scratch((LAYERS, 2, 8, NET_WIDTH), F32),
            scratch((2, grad_rows, NET_WIDTH), F32),
            scratch((grad_rows, NET_WIDTH), F32),
            scratch((grad_rows, NET_WIDTH), BF16),
            scratch((grad_rows, NET_WIDTH), BF16),
            scratch((2, grad_rows, NET_WIDTH), F32),
            peers, peers, peers, peers, peers, peers, peers, peers, peers, peers,
            sem((3, LAYERS + 1)),
            sem((3, LAYERS + 1)),
        ],
        compiler_params=pltpu.CompilerParams(
            collective_id=0, has_side_effects=True, vmem_limit_bytes=189 * 2**18 + 2 * wide_rows * sample_count
        ),
        cost_estimate=pl.CostEstimate(flops=0, bytes_accessed=50000 * sample_count, transcendentals=0),
        name="step",
    )(*placed)
    whole = shape(params.shape, F32)
    new_params, new_first, new_second, loss, *tables = pl.pallas_call(
        update_kernel,
        out_shape=[whole] * 3 + [shape((1, ray_rows), F32)] + [table_shape] * 3,
        in_specs=[VMEM] * 8,
        out_specs=[HBM] * 7,
        scratch_shapes=[scratch(params.shape, F32)] * 3 + [sem((3, 4)), sem((4,))],
        compiler_params=pltpu.CompilerParams(vmem_limit_bytes=16 * 2**20),
        name="update",
    )(
        param_grad, master, first_moment, second_moment, loss,
        new_table, new_table_first, new_table_second,
    )
    return (loss.reshape(ray_rows), new_params, new_first, new_second, *tables)


def solution(mesh):
    both = ("expert", "dp")
    return jax.shard_map(
        shards,
        mesh=mesh,
        in_specs=(
            P(both, None, None), P(both, None), P(None, both), P(both), P(both, None),
            P(both, None), P(both),
            P("expert", None, None), P("expert", None, None), P("expert", None, None),
            P(both, None), P(both, None), P(both, None),
        ),
        out_specs=(
            P(both),
            P("expert", None, None), P("expert", None, None), P("expert", None, None),
            P(both, None), P(both, None), P(both, None),
        ),
        check_vma=False,
    )
```

```python
import functools
import math

import jax
import jax.numpy as jnp
from jax import lax
from jax.experimental import pallas as pl
from jax.experimental.pallas import tpu as pltpu
from jax.sharding import PartitionSpec as P

NET_WIDTH = 256
CODE_WIDTH = 64
ENC_WIDTH = 64
LAYERS = 4
SAMPLES = 32
HEAD_ROW = ENC_WIDTH + (LAYERS - 1) * NET_WIDTH
LANES = 128

BETA_ONE = 0.9
BETA_TWO = 0.999
LEARN_RATE = 0.001
ADAM_EPS = 1e-08
CORRECT_ONE = 1.0 - 0.9**10
CORRECT_TWO = 1.0 - 0.999**10

MESH = pl.DeviceIdType.MESH
VMEM = pl.BlockSpec(memory_space=pltpu.VMEM)
HBM = pl.BlockSpec(memory_space=pltpu.HBM)
F32 = jnp.float32
BF16 = jnp.bfloat16
NN = (((1,), (0,)), ((), ()))
NT = (((1,), (1,)), ((), ()))
TN = (((0,), (0,)), ((), ()))


def dot(left, right, dims=NN, precision=None):
    return lax.dot_general(left, right, dims, precision=precision, preferred_element_type=F32)


def exact(left, right, dims=NN):
    return dot(left, right, dims, lax.Precision.HIGHEST)


def adam_update(param_now, gradient, moment_one, moment_two):
    new_one = BETA_ONE * moment_one + (1.0 - BETA_ONE) * gradient
    new_two = BETA_TWO * moment_two + (1.0 - BETA_TWO) * gradient * gradient
    update = LEARN_RATE * (new_one / CORRECT_ONE) / (jnp.sqrt(new_two / CORRECT_TWO) + ADAM_EPS)
    return (param_now - update, new_one, new_two)


def iota(shape, dim):
    return lax.broadcasted_iota(jnp.int32, shape, dim)


def lane_block(index):
    return pl.ds(pl.multiple_of(index * LANES, LANES), LANES)


def rows_of(index, count, align=8):
    return pl.ds(pl.multiple_of(index * count, align), count)


def place_kernel(
    groups, cap, cap_up, cell_hbm, rank_hbm, feat_hbm, params_hbm, *refs,
):
    others = refs[:9]
    out_ref, master, cell_ref, rank_ref = refs[9:13]
    other_outs = refs[13:22]
    feat, rows, table, counts, slot_vec, slot, load_sems, slot_sem = refs[22:]
    pairs = [(cell_hbm, cell_ref), (rank_hbm, rank_ref), (feat_hbm, feat), (params_hbm, master)]
    pairs += list(zip(others, other_outs))
    loads = [
        pltpu.make_async_copy(source, target, load_sems.at[n])
        for n, (source, target) in enumerate(pairs)
    ]
    for load in loads:
        load.start()
    loads[0].wait()
    loads[1].wait()
    cell = cell_ref[...]
    rank = rank_ref[...]
    live = rank >= 0
    slot_vec[...] = jnp.where(live, cell * cap_up + rank, 2 * groups * cap_up)
    scalars = pltpu.make_async_copy(slot_vec, slot, slot_sem)
    scalars.start()
    kind = jnp.where(live, cell, -1)

    def count(g, carry):
        parts = [
            jnp.sum(jnp.where(kind == 8 * g + j, 1.0, 0.0), axis=0, keepdims=True)
            for j in range(8)
        ]
        total = jnp.sum(jnp.concatenate(parts, axis=0), axis=1, keepdims=True)
        counts[rows_of(g, 8), :] = jnp.broadcast_to(total, (8, LANES))
        return carry

    lax.fori_loop(0, 2 * groups // 8, count, 0)
    loads[2].wait()

    def turn(index, carry):
        for inner in range(4):
            i = index * 4 + inner
            block = feat[i].astype(F32)
            rows[lane_block(i), :] = jnp.concatenate([block, block], axis=0).T
        return carry

    lax.fori_loop(0, SAMPLES // 4, turn, 0)
    scalars.wait()
    for i in range(SAMPLES):

        def move(r, carry):
            table[pl.ds(slot[i, r], 1), :] = rows[pl.ds(i * LANES + r, 1), :]
            return carry

        lax.fori_loop(0, LANES, move, 0, unroll=True)
    low = iota((1, LANES), 1) < ENC_WIDTH
    position = iota((cap, LANES), 0).astype(F32)

    def pack(g, carry):
        first = table[pl.ds(pl.multiple_of(2 * g * cap_up, LANES), cap), :]
        second = table[pl.ds(pl.multiple_of((2 * g + 1) * cap_up, LANES), cap), :]
        limit = jnp.where(low, counts[pl.ds(2 * g, 1), :], counts[pl.ds(2 * g + 1, 1), :])
        value = jnp.where(low, first, second)
        out_ref[g] = jnp.where(position < limit, value, 0.0).astype(BF16)
        return carry

    lax.fori_loop(0, groups, pack, 0)
    for load in loads[3:]:
        load.wait()


def flipped(me, k, groups):
    peer = 0
    bit = 1
    while bit < groups:
        peer = peer + bit * lax.rem(lax.div(me, bit) + lax.div(k, bit), 2)
        bit *= 2
    return peer


def layer_matrix(wt, m0, h, layer):
    if layer == 0:
        return m0[h]
    start = ENC_WIDTH + (layer - 1) * NET_WIDTH
    return wt[h, start : start + NET_WIDTH, :]


def tail_rows(wt, h):
    return wt[h, HEAD_ROW : HEAD_ROW + 16, :]


def prefix(value, row, backwards):
    step = 1
    while step < SAMPLES:
        if backwards:
            moved = jnp.where(row < SAMPLES - step, pltpu.roll(value, SAMPLES - step, 0), 0.0)
        else:
            moved = jnp.where(row >= step, pltpu.roll(value, step, 0), 0.0)
        value = value + moved
        step *= 2
    return value


def step_kernel(
    groups, cap, cap_up,
    disp, master, cell_ref, rank_ref, spacing_ref, length_ref, target_ref, image_ref,
    code_ref, first_ref, second_ref, moment_one, moment_two,
    params_out, one_out, two_out, loss_out, code_out, first_out, second_out,
    wt, m0, turned, head, recv, act, act_t, feat_t, pre,
    raw_msg, back, tail_msg, tails, queries, shift, mix, eight, keys, spots,
    cot_msg, cot_in, code_msg, code_in, cot_sum, bias, wide_grad, grad, half_out, half_in, sum_out, sum_in, full,
    s_out, r_out, s_back, r_back, s_tail, r_tail, s_cot, r_cot, s_code, r_code,
    s_sum, r_sum,
):
    tiles = cap_up // LANES
    batch = LANES // math.gcd(cap, LANES)
    parts = [(0, cap)]
    me = lax.axis_index("expert")
    my_dp = lax.axis_index("dp")
    core = lax.rem(my_dp, 2)
    near = my_dp + 1 - 2 * core
    far = my_dp + 2 - 4 * lax.rem(lax.div(my_dp, 2), 2)
    barrier = pltpu.get_barrier_semaphore()

    def greet(k, carry):
        pl.semaphore_signal(
            barrier, 1, device_id={"expert": lax.rem(me + k, groups)}, device_id_type=MESH
        )
        return carry

    lax.fori_loop(1, groups, greet, 0)
    for peer in (near, far):
        pl.semaphore_signal(barrier, 1, device_id={"dp": peer}, device_id_type=MESH)

    def turn_of(j):
        return j

    def block_rows(k):
        return rows_of(k, cap, 16)

    def peer_copy(k, source, target, sends, receives):
        return pltpu.make_async_remote_copy(
            source, target, sends.at[k], receives.at[k],
            device_id={"expert": flipped(me, k, groups)}, device_id_type=MESH,
        )

    def part_rows(k, part):
        start, size = parts[part]
        return pl.ds(pl.multiple_of(k * cap + start, 16), size)

    def out_copy(k, part):
        start, size = parts[part]
        return pltpu.make_async_remote_copy(
            disp.at[flipped(me, k, groups), pl.ds(start, size)], recv.at[part_rows(k, part)],
            s_out.at[part, k], r_out.at[part, k],
            device_id={"expert": flipped(me, k, groups)}, device_id_type=MESH,
        )

    def back_copy(k):
        return peer_copy(k, raw_msg.at[k], back.at[me], s_back, r_back)

    def tail_copy(k):
        return peer_copy(k, tail_msg, tails.at[me], s_tail, r_tail)

    def cot_copy(k):
        return peer_copy(k, cot_msg.at[flipped(me, k, groups)], cot_in.at[k], s_cot, r_cot)

    def code_copy(k):
        return peer_copy(k, code_msg.at[flipped(me, k, groups)], code_in.at[k], s_code, r_code)

    def each(body):
        def turn(j, carry):
            body(turn_of(j))
            return carry

        lax.fori_loop(1, groups, turn, 0)

    spot = iota((4, LANES), 0) == iota((4, LANES), 1)
    lane = iota((4, LANES), 1)
    for h in range(2):
        tail = tail_rows(master, h).astype(BF16).astype(F32)
        column = jnp.sum(jnp.where(spot, tail[8:9, 0:LANES], 0.0), axis=1, keepdims=True)
        tail_msg[4 * h : 4 * h + 4, :] = jnp.where(
            lane < CODE_WIDTH, tail[4:8, 0:LANES], jnp.where(lane == CODE_WIDTH, column, 0.0)
        )
    tails[me] = tail_msg[...]
    pl.semaphore_wait(barrier, groups + 1)
    each(lambda k: tail_copy(k).start())
    def send(k):
        for part in range(len(parts)):
            out_copy(k, part).start()

    each(send)
    recv[block_rows(0), :] = disp[me]
    wt[...] = master[...].astype(BF16)
    m0[...] = jnp.zeros_like(m0)
    head[...] = jnp.zeros_like(head)
    ones = jnp.ones((16, recv.shape[0]), BF16)
    feat_t[LANES:, :] = ones
    for layer in range(LAYERS - 1):
        for h in range(2):
            act_t[layer, h, NET_WIDTH:, :] = ones
    for h in range(2):
        m0[h, ENC_WIDTH * h : ENC_WIDTH * (h + 1), :] = wt[h, 0:ENC_WIDTH, :]
        head[h, 4 * h : 4 * h + 4, :] = tail_rows(wt, h).astype(F32)[0:4]

    def process(k, part):
        start, size = parts[part]
        block = part_rows(k, part)
        features = recv[block, :]
        biases = [tail_rows(wt, h).astype(F32) for h in range(2)]
        current = [features, features]
        for layer in range(LAYERS):
            for h in range(2):
                preact = dot(current[h], layer_matrix(wt, m0, h, layer))
                preact = preact + biases[h][9 + layer : 10 + layer, :]
                current[h] = jnp.maximum(preact, 0.0).astype(BF16)
                act[layer, h, block, :] = current[h]
        for h in range(2):
            raw = dot(tail_rows(wt, h), current[h], NT)
            raw_msg[k, 4 * h : 4 * h + 4, start : start + size] = raw[0:4]

    for part in range(len(parts)):
        process(0, part)
    back[me] = raw_msg[0]

    for h in range(2):
        for layer in range(1, LAYERS):
            matrix = layer_matrix(wt, m0, h, layer)
            turned[layer - 1, h] = matrix.astype(F32).T.astype(BF16)

    cell = cell_ref[...]
    rank = rank_ref[...]
    row = iota((SAMPLES, LANES), 0)
    live = row < length_ref[...]
    place = jnp.where(live, rank, 0)
    tile = lax.div(place, LANES)
    lane_index = place - tile * LANES
    key = jnp.where(live, cell * tiles + tile, -1)
    table_rows = code_ref.shape[0]
    block_index = me * lax.axis_size("dp") + my_dp
    pick = (
        iota((table_rows, LANES), 0) == image_ref[...] - block_index * table_rows
    ).astype(F32)
    ray_code = exact(code_ref[...].astype(BF16).astype(F32), pick, TN)

    keys[...] = key.astype(F32)
    eight[0:SAMPLES, :] = lane_index.astype(F32)
    slot_lane = iota((LANES, LANES), 0).astype(F32)

    def spread(i, carry):
        line = jnp.broadcast_to(eight[pl.ds(i, 1), :], (LANES, LANES))
        spots[:, lane_block(i)] = jnp.where(line == slot_lane, 1.0, 0.0).astype(BF16)
        return carry

    lax.fori_loop(0, SAMPLES, spread, 0)

    def transpose(c):
        rows = rows_of(c, batch * cap, 16)
        lanes = pl.ds(pl.multiple_of(c * batch * cap, LANES), batch * cap)
        feat_t[0:LANES, lanes] = recv[rows, :].T
        for layer in range(LAYERS - 1):
            for h in range(2):
                act_t[layer, h, 0:NET_WIDTH, lanes] = act[layer, h, rows, :].T

    def receive(k, carry):
        for part in range(len(parts)):
            out_copy(k, part).wait_recv()
            process(k, part)
        back_copy(k).start()
        return carry

    def receive_batch(c, carry):
        lax.fori_loop(c * batch, (c + 1) * batch, receive, 0)
        transpose(c)
        return carry

    def receive_pair(pair, carry):
        for part in range(len(parts)):

            def arrive(k, inner):
                out_copy(k, part).wait_recv()
                process(k, part)
                if part == len(parts) - 1:
                    back_copy(k).start()
                return inner

            lax.fori_loop(2 * pair, 2 * pair + 2, arrive, 0)
        transpose(2 * pair)
        transpose(2 * pair + 1)
        return carry

    if batch == 1:
        transpose(0)
        receive(1, 0)
        transpose(1)
        lax.fori_loop(1, groups // 2, receive_pair, 0)
    else:
        lax.fori_loop(1, batch, receive, 0)
        transpose(0)
        lax.fori_loop(1, groups // batch, receive_batch, 0)

    each(lambda k: tail_copy(k).wait_recv())

    def collect(g, carry):
        queries[rows_of(g, 8), :] = tails[g, :, 0:CODE_WIDTH]
        shift[rows_of(g, 8), :] = jnp.broadcast_to(
            tails[g, :, CODE_WIDTH : CODE_WIDTH + 1], (8, LANES)
        )
        return carry

    lax.fori_loop(0, groups, collect, 0)
    mix[...] = exact(queries[...], ray_code) + shift[...]
    zero = jnp.zeros((SAMPLES, LANES), F32)

    def add_code(g, codes):
        part = mix[rows_of(g, 8), :]
        codes = list(codes)
        for h in range(2):
            hit = cell == 2 * g + h
            for c in range(4):
                j = 4 * h + c
                codes[c] = jnp.where(hit, part[j : j + 1, :], codes[c])
        return tuple(codes)

    codes = lax.fori_loop(0, groups, add_code, (zero,) * 4)

    def take(g, raws):
        raws = list(raws)
        for t in range(tiles):
            piece = back[g, :, t * LANES : (t + 1) * LANES]
            for h in range(2):
                hit = key == (2 * g + h) * tiles + t
                for c in range(4):
                    j = 4 * h + c
                    line = jnp.broadcast_to(piece[j : j + 1, :], (SAMPLES, LANES))
                    found = jnp.take_along_axis(line, lane_index, axis=1)
                    raws[c] = jnp.where(hit, found, raws[c])
        return tuple(raws)

    raws = take(me, (zero,) * 4)

    def take_next(j, raws):
        k = turn_of(j)
        back_copy(k).wait_recv()
        return take(flipped(me, k, groups), raws)

    raws = lax.fori_loop(1, groups, take_next, raws)
    raws = [jnp.where(live, raws[c] + codes[c], 0.0) for c in range(4)]
    spacing = spacing_ref[...]
    density = jnp.maximum(raws[0], 0.0) + jnp.log1p(jnp.exp(-jnp.abs(raws[0])))
    colors = [jax.nn.sigmoid(raw) for raw in raws[1:]]
    tau = jnp.where(live, density * spacing, 0.0)
    before = prefix(tau, row, False) - tau
    through = jnp.exp(-before)
    fade = jnp.exp(-tau)
    weight = through * (1.0 - fade)
    gaps = [
        jnp.sum(weight * colors[c], axis=0, keepdims=True) - target_ref[c : c + 1, :]
        for c in range(3)
    ]
    loss_out[...] = 0.5 * (gaps[0] * gaps[0] + gaps[1] * gaps[1] + gaps[2] * gaps[2])
    pull = gaps[0] * colors[0] + gaps[1] * colors[1] + gaps[2] * colors[2]
    gain = pull * weight
    after = prefix(gain, row, True) - gain
    tau_grad = pull * through * fade - after
    grads = [tau_grad * spacing * jax.nn.sigmoid(raws[0])]
    for c in range(3):
        grads.append(gaps[c] * weight * colors[c] * (1.0 - colors[c]))
    for c in range(4):
        cot = jnp.where(live, grads[c], 0.0).astype(BF16).astype(F32)
        eight[pl.ds(c, SAMPLES, 8), :] = cot
        eight[pl.ds(4 + c, SAMPLES, 8), :] = cot
    mix[...] = jnp.zeros_like(mix)
    member = lax.div(iota((8, LANES), 0), 4) * tiles

    wide_rows = tiles * groups * 8
    strips = SAMPLES // 2

    def widen(index, carry):
        sums = [0.0] * groups
        for n in range(2):
            i = 2 * index + n
            value = eight[rows_of(i, 8), :]
            line = jnp.broadcast_to(keys[pl.ds(i, 1), :], (8, LANES))
            for t in range(tiles):
                for pair in range(groups // 2):
                    both = []
                    for g in (2 * pair, 2 * pair + 1):
                        want = (member + (2 * g * tiles + t)).astype(F32)
                        chosen = jnp.where(line == want, value, 0.0)
                        sums[g] = sums[g] + chosen
                        both.append(chosen)
                    start = index * wide_rows + (t * groups + 2 * pair) * 8
                    pre[pl.ds(pl.multiple_of(start, 16), 16), n * LANES : (n + 1) * LANES] = (
                        jnp.concatenate(both, axis=0).astype(BF16)
                    )
        for g in range(groups):
            mix[8 * g : 8 * g + 8, :] += sums[g]
        return carry

    lax.fori_loop(0, strips, widen, 0)
    slots = sum(
        dot(
            pre[n * wide_rows : (n + 1) * wide_rows, :],
            spots[:, 2 * n * LANES : 2 * (n + 1) * LANES], NT,
        )
        for n in range(strips)
    )
    for t in range(tiles):
        for g in range(groups):
            start = (t * groups + g) * 8
            cot_msg[g, :, t * LANES : (t + 1) * LANES] = slots[start : start + 8].astype(BF16)
    each(lambda k: cot_copy(k).start())
    cot_in[0] = cot_msg[me]

    totals = mix[...]
    query_grad = exact(totals, ray_code, NT)
    for g in range(groups):
        code_msg[g, :, 0:CODE_WIDTH] = query_grad[8 * g : 8 * g + 8]
        code_msg[g, :, CODE_WIDTH:] = jnp.zeros((8, LANES - CODE_WIDTH), F32)
    each(lambda k: code_copy(k).start())
    code_in[0] = code_msg[me]
    table_grad = exact(exact(totals, pick, NT), queries[...], TN)
    new_code, new_first, new_second = adam_update(
        code_ref[...], table_grad, first_ref[...], second_ref[...]
    )
    code_out[...] = new_code
    first_out[...] = new_first
    second_out[...] = new_second

    piece_rows = NET_WIDTH // 2
    starts = [0] + list(range(ENC_WIDTH, HEAD_ROW + 1, piece_rows)) + [HEAD_ROW + 16]
    chunks = [pl.ds(starts[j], starts[j + 1] - starts[j]) for j in range(len(starts) - 1)]
    tail_chunk = len(chunks) - 1

    def chunks_of(layer):
        return [0] if layer == 0 else [2 * layer - 1, 2 * layer]

    def near_copy(j):
        return pltpu.make_async_remote_copy(
            half_out.at[chunks[j]], half_in.at[chunks[j]],
            s_sum.at[0, j], r_sum.at[0, j], device_id={"dp": near}, device_id_type=MESH,
        )

    def far_copy(j):
        return pltpu.make_async_remote_copy(
            sum_out.at[chunks[j]], sum_in.at[chunks[j]],
            s_sum.at[1, j], r_sum.at[1, j], device_id={"dp": far}, device_id_type=MESH,
        )

    def full_copy(j, which):
        return pltpu.make_async_remote_copy(
            full.at[which, chunks[j]], full.at[which, chunks[j]],
            s_sum.at[2, j], r_sum.at[2, j], device_id={"dp": near}, device_id_type=MESH,
        )

    def second_stage(j):
        near_copy(j).wait_recv()
        rows = chunks[j]
        sum_out[rows, :] = (grad[rows, :] + half_in[rows, :].astype(F32)).astype(BF16)
        far_copy(j).start()

    def third_stage(j):
        far_copy(j).wait_recv()
        rows = chunks[j]
        total = sum_out[rows, :].astype(F32) + sum_in[rows, :].astype(F32)
        full[core, rows, :] = total.astype(BF16)
        full_copy(j, core).start()

    top = LAYERS - 1
    heads_bf = [head[h].astype(BF16) for h in range(2)]
    cot_sum[...] = jnp.zeros_like(cot_sum)

    all_rows = recv.shape[0]

    def pre_rows(layer, h, start=0, size=all_rows):
        first = (layer % 2 * 2 + h) * all_rows + start
        return pl.ds(pl.multiple_of(first, 16), size)

    def mask_store(layer, h, start, size, up):
        up = up.astype(BF16)
        rows = pl.ds(pl.multiple_of(start, 16), size)
        pre[pre_rows(layer, h, start, size), :] = jnp.where(
            act[layer, h, rows, :] > 0, up, jnp.zeros_like(up)
        )

    def first_back(k, carry):
        block = block_rows(k)
        cot = cot_in[k, :, 0:cap]
        sums = []
        for h in range(2):
            mask_store(top, h, k * cap, cap, dot(cot, heads_bf[h], TN))
            sums.append(carry[h] + dot(cot, act[top, h, block, :]))
        cot_sum[...] += jnp.broadcast_to(
            jnp.sum(cot.astype(F32), axis=1, keepdims=True), (8, LANES)
        )
        return tuple(sums)

    def next_back(j, carry):
        k = turn_of(j)
        cot_copy(k).wait_recv()
        return first_back(k, carry)

    zeros = jnp.zeros((8, NET_WIDTH), F32)
    hidden = lax.fori_loop(1, groups, next_back, first_back(0, (zeros, zeros)))

    for layer in reversed(range(LAYERS)):
        if layer < top:
            for h in range(2):
                if h == 1:
                    for j in chunks_of(layer + 1):
                        second_stage(j)
                up = dot(pre[pre_rows(layer + 1, h), :], turned[layer, h])
                mask_store(layer, h, 0, all_rows, up)

        if layer == 0:
            for h in range(2):
                value = dot(feat_t[...], pre[pre_rows(0, h), :])
                bias[0, h, 0:1, :] = value[LANES : LANES + 1]
                wide_grad[h] = value[ENC_WIDTH * h : ENC_WIDTH * (h + 1)]
            half_out[0:ENC_WIDTH, :] = wide_grad[1 - core].astype(BF16)
            near_copy(0).start()
            grad[0:ENC_WIDTH, :] = wide_grad[core]
        else:
            rows = pl.ds(starts[2 * layer - 1], NET_WIDTH)
            for h in (1 - core, core):
                value = dot(act_t[layer - 1, h], pre[pre_rows(layer, h), :])
                bias[layer, h, 0:1, :] = value[NET_WIDTH : NET_WIDTH + 1]
                if h is core:
                    grad[rows, :] = value[0:NET_WIDTH]
                else:
                    half_out[rows, :] = value[0:NET_WIDTH].astype(BF16)
                    for j in chunks_of(layer):
                        near_copy(j).start()
        if layer < top - 1:
            for j in chunks_of(layer + 2):
                third_stage(j)

    def add_codes(k, carry):
        code_copy(k).wait_recv()
        return carry + code_in[k]

    code_sum = lax.fori_loop(1, groups, add_codes, code_in[0])
    codes = jnp.concatenate([code_sum, jnp.zeros((8, NET_WIDTH - LANES), F32)], axis=1)
    spot = iota((8, LANES), 0) == iota((8, LANES), 1)
    cot_row = jnp.sum(jnp.where(spot, cot_sum[...], 0.0), axis=0, keepdims=True)
    lane = iota((1, LANES), 1)
    for h in range(2):
        line = cot_row if h == 0 else pltpu.roll(cot_row, LANES - 4, 1)
        line = jnp.where(lane < 4, line, 0.0)
        line = jnp.concatenate([line, jnp.zeros((1, NET_WIDTH - LANES), F32)], axis=1)
        wide_grad[h, 0:16, :] = jnp.concatenate(
            [hidden[h][4 * h : 4 * h + 4], codes[4 * h : 4 * h + 4], line]
            + [bias[layer, h, 0:1, :] for layer in range(LAYERS)]
            + [jnp.zeros((7 - LAYERS, NET_WIDTH), F32)],
            axis=0,
        )
    def finish(j):
        full_copy(j, 1 - core).wait_recv()
        start = starts[j]

        def update(index, carry):
            spot = (slice(None), pl.ds(pl.multiple_of(start + index * 16, 16), 16), slice(None))
            values = adam_update(master[spot], full[spot].astype(F32), moment_one[spot], moment_two[spot])
            for target, value in zip((params_out, one_out, two_out), values):
                target[spot] = value
            return carry

        lax.fori_loop(0, (starts[j + 1] - start) // 16, update, 0)

    tail = chunks[tail_chunk]
    half_out[tail, :] = wide_grad[1 - core, 0:16, :].astype(BF16)
    near_copy(tail_chunk).start()
    grad[tail, :] = wide_grad[core, 0:16, :]
    second_stage(0)
    second_stage(tail_chunk)
    late = [chunks_of(1)[0], chunks_of(1)[1], 0, tail_chunk]
    early = [chunks_of(3), chunks_of(2)[0:1], chunks_of(2)[1:], []]
    for n in range(4):
        for j in early[n]:
            finish(j)
        third_stage(late[n])
        if n > 1:
            finish(late[n - 2])
    finish(0)
    finish(tail_chunk)

    def drain(k):
        for part in range(len(parts)):
            out_copy(k, part).wait_send()
        for copy in (tail_copy, back_copy, cot_copy, code_copy):
            copy(k).wait_send()

    each(drain)
    for j in range(len(chunks)):
        near_copy(j).wait_send()
        far_copy(j).wait_send()
        full_copy(j, core).wait_send()


def store_kernel(*refs):
    count = len(refs) // 2
    sems = refs[2 * count]
    copies = [
        pltpu.make_async_copy(refs[n], refs[count + n], sems.at[n]) for n in range(count)
    ]
    for copy in copies:
        copy.start()
    for copy in copies:
        copy.wait()


def shards(
    features, spacing, targets, ray_length, cell_id, slot_rank, image_id,
    params, first_moment, second_moment, code_table, table_first, table_second,
):
    ray_rows = features.shape[0]
    sample_count = ray_rows * SAMPLES
    groups = lax.axis_size("expert")
    experts_all = params.shape[0] * groups
    cap = 2 * (sample_count * 3 // 4 // experts_all)
    cap_up = -(-cap // LANES) * LANES
    tiles = cap_up // LANES
    slots_up = experts_all * cap_up
    shape = jax.ShapeDtypeStruct
    scratch = pltpu.VMEM
    sem = pltpu.SemaphoreType.DMA
    smalls = [
        spacing.T, ray_length[None, :], targets, image_id[None, :],
        code_table, table_first, table_second, first_moment, second_moment,
    ]
    inputs = [cell_id.T, slot_rank.T, features.transpose(1, 2, 0), params] + smalls
    inputs = [pltpu.with_memory_space_constraint(value, pltpu.HBM) for value in inputs]
    like = lambda value: shape(value.shape, value.dtype)
    placed = pl.pallas_call(
        functools.partial(place_kernel, groups, cap, cap_up),
        out_shape=[
            shape((groups, cap, LANES), BF16),
        ] + [like(value) for value in [params] + inputs[0:2] + smalls],
        in_specs=[HBM] * len(inputs),
        out_specs=[VMEM] * (4 + len(smalls)),
        scratch_shapes=[
            scratch((SAMPLES, ENC_WIDTH, ray_rows), BF16),
            scratch((sample_count, LANES), F32),
            scratch((slots_up + 8, LANES), F32),
            scratch((experts_all, LANES), F32),
            scratch((SAMPLES, LANES), jnp.int32),
            pltpu.SMEM((SAMPLES, LANES), jnp.int32),
            sem((len(inputs),)), sem,
        ],
        compiler_params=pltpu.CompilerParams(vmem_limit_bytes=12 * 2**20),
        cost_estimate=pl.CostEstimate(flops=0, bytes_accessed=6000 * sample_count, transcendentals=0),
        name="place",
    )(*inputs)
    all_rows = groups * cap
    grad_rows = params.shape[1]
    table_shape = shape(code_table.shape, F32)
    peers = sem((groups,))
    step_vmem = 81 * 2**19 + groups * 48 * 2**10
    whole = shape(params.shape, F32)
    results = pl.pallas_call(
        functools.partial(step_kernel, groups, cap, cap_up),
        out_shape=[whole] * 3 + [shape((1, ray_rows), F32)] + [table_shape] * 3,
        in_specs=[VMEM] * 13,
        out_specs=[VMEM] * 7,
        scratch_shapes=[
            scratch(params.shape, BF16),
            scratch((2, LANES, NET_WIDTH), BF16),
            scratch((LAYERS - 1, 2, NET_WIDTH, NET_WIDTH), BF16),
            scratch((2, 8, NET_WIDTH), F32),
            scratch((all_rows, LANES), BF16),
            scratch((LAYERS, 2, all_rows, NET_WIDTH), BF16),
            scratch((LAYERS - 1, 2, NET_WIDTH + 16, all_rows), BF16),
            scratch((LANES + 16, all_rows), BF16),
            scratch((4 * all_rows, NET_WIDTH), BF16),
            scratch((groups, 8, cap_up), F32),
            scratch((groups, 8, cap_up), F32),
            scratch((8, LANES), F32),
            scratch((groups, 8, LANES), F32),
            scratch((8 * groups, CODE_WIDTH), F32),
            scratch((8 * groups, LANES), F32),
            scratch((8 * groups, LANES), F32),
            scratch((8 * SAMPLES, LANES), F32),
            scratch((SAMPLES, LANES), F32),
            scratch((LANES, sample_count), BF16),
            scratch((groups, 8, cap_up), BF16),
            scratch((groups, 8, cap_up), BF16),
            scratch((groups, 8, LANES), F32),
            scratch((groups, 8, LANES), F32),
            scratch((8, LANES), F32),
            scratch((LAYERS, 2, 8, NET_WIDTH), F32),
            scratch((2, ENC_WIDTH, NET_WIDTH), F32),
            scratch((grad_rows, NET_WIDTH), F32),
            scratch((grad_rows, NET_WIDTH), BF16),
            scratch((grad_rows, NET_WIDTH), BF16),
            scratch((grad_rows, NET_WIDTH), BF16),
            scratch((grad_rows, NET_WIDTH), BF16),
            scratch((2, grad_rows, NET_WIDTH), BF16),
            sem((2, groups)), sem((2, groups)),
            peers, peers, peers, peers, peers, peers, peers, peers,
            sem((3, 2 * LAYERS)),
            sem((3, 2 * LAYERS)),
        ],
        compiler_params=pltpu.CompilerParams(
            collective_id=0, has_side_effects=True, vmem_limit_bytes=step_vmem
        ),
        cost_estimate=pl.CostEstimate(flops=0, bytes_accessed=50000 * sample_count, transcendentals=0),
        name="step",
    )(*placed)
    new_params, new_first, new_second, loss, *tables = pl.pallas_call(
        store_kernel,
        out_shape=[shape(value.shape, value.dtype) for value in results],
        in_specs=[VMEM] * 7,
        out_specs=[HBM] * 7,
        scratch_shapes=[sem((7,))],
        compiler_params=pltpu.CompilerParams(vmem_limit_bytes=2**20),
        name="store",
    )(*results)
    return (loss.reshape(ray_rows), new_params, new_first, new_second, *tables)


def solution(mesh):
    both = ("expert", "dp")
    return jax.shard_map(
        shards,
        mesh=mesh,
        in_specs=(
            P(both, None, None), P(both, None), P(None, both), P(both), P(both, None),
            P(both, None), P(both),
            P("expert", None, None), P("expert", None, None), P("expert", None, None),
            P(both, None), P(both, None), P(both, None),
        ),
        out_specs=(
            P(both),
            P("expert", None, None), P("expert", None, None), P("expert", None, None),
            P(both, None), P(both, None), P(both, None),
        ),
        check_vma=False,
    )
```
